32 devices in a mesh: row: 2 (over y), col: 16 (over z, x, core).
Axes of the slice: x: 2, y: 2, z: 4, core: 2. Of those that a mesh axis runs over, the one named last changes fastest.
Arguments:
- tokens: bfloat16 [25088, 1024], P(('col', 'row')), may hold values from -6 to 6
- w_qkv: bfloat16 [1024, 3072], P('row', 'col'), may hold values from -0.1875 to 0.1875
- w_proj: bfloat16 [1024, 1024], P('row', 'col'), may hold values from -6 to 6
- w_fc1: bfloat16 [1024, 4096], P('row', 'col'), may hold values from -0.1875 to 0.1875
- w_fc2: bfloat16 [4096, 1024], P('row', 'col'), may hold values from -0.09375 to 0.09375
- ln1_gain: bfloat16 [1024], P(('col', 'row')), may hold values from 0.099609375 to 1.8984375
- ln1_bias: bfloat16 [1024], P(('col', 'row')), may hold values from -6 to 6
- q_bias: bfloat16 [1024], P(('col', 'row')), may hold values from -6 to 6
- v_bias: bfloat16 [1024], P(('col', 'row')), may hold values from -0.4375 to 0.4375
- proj_bias: bfloat16 [1024], P(('col', 'row')), may hold values from -6 to 6
- ln2_gain: bfloat16 [1024], P(('col', 'row')), may hold values from 0.099609375 to 1.8984375
- ln2_bias: bfloat16 [1024], P(('col', 'row')), may hold values from -6 to 6
- fc1_bias: bfloat16 [4096], P(('col', 'row')), may hold values from -6 to 6
- fc2_bias: bfloat16 [1024], P(('col', 'row')), may hold values from -6 to 6
- cotangent: float32 [25088, 1024], P(('col', 'row')), may hold values from -6 to 6
Outputs:
- output: bfloat16 [25088, 1024], P(('col', 'row'))
- grad_tokens: float32 [25088, 1024], P(('col', 'row'))
- grad_qkv: float32 [1024, 3072], P('row', 'col')
- grad_proj: float32 [1024, 1024], P('row', 'col')
- grad_fc1: float32 [1024, 4096], P('row', 'col')
- grad_fc2: float32 [4096, 1024], P('row', 'col')
- grad_ln1_gain: float32 [1024], P(('col', 'row'))
- grad_ln1_bias: float32 [1024], P(('col', 'row'))
- grad_q_bias: float32 [1024], P(('col', 'row'))
- grad_v_bias: float32 [1024], P(('col', 'row'))
- grad_proj_bias: float32 [1024], P(('col', 'row'))
- grad_ln2_gain: float32 [1024], P(('col', 'row'))
- grad_ln2_bias: float32 [1024], P(('col', 'row'))
- grad_fc1_bias: float32 [4096], P(('col', 'row'))
- grad_fc2_bias: float32 [1024], P(('col', 'row'))
The draws below stay inside these ranges and needn't reach their ends.
All inputs are finite; a program needn't handle non-finite values.
Results may differ from the reference program's by a relative error of at most 0.019.
Values may be sent and summed in bfloat16 or wider, within the bound.
No kernel may reach another device: no remote copies, remote signals or barrier semaphores. Data moves between devices by JAX's collectives and lax.ppermute only.
A program may use at most 448 MiB of HBM per device.

```python
import jax
import jax.numpy as jnp
from jax import lax

D = 1024
H = 16
HD = 64
FF = 4096
LEN = 1568
CLIPS = 16
TOKENS = 25088


def spiked(values, own_key, source, target, parts, factor):
    def block_of(position):
        return (jnp.arange(values.shape[position]) // (values.shape[position] // parts)).reshape((-1,) + (1,) * (values.ndim - 1 - position))

    first = jax.random.permutation(own_key, parts)[block_of(target)]
    far = (block_of(target) + parts // 2) % parts
    return jnp.where((block_of(source) == first) | (block_of(source) == far), factor * values, values)


def block_levels(own_key, dims, cuts, low, top_value):
    loudness = 1.0
    for position, shards_of in cuts:
        steps = jax.random.uniform(jax.random.fold_in(jax.random.fold_in(own_key, 6), position), (shards_of,), jnp.float32, low / len(cuts), top_value / len(cuts))
        loudness = loudness * jnp.repeat(jnp.exp(steps), dims[position] // shards_of).reshape((-1,) + (1,) * (len(dims) - 1 - position))
    return loudness


def bell_draw(rng, extent, scale, limit, shards=(), dtype=jnp.bfloat16):
    factor_of = block_levels(rng, extent, shards, -0.22, 0.18) if shards else 1.0
    values = jax.random.normal(rng, extent, jnp.float32) * scale * factor_of
    return jnp.minimum(jnp.maximum(values, -limit), limit).astype(dtype)


def noise_with(own_key, dims, deviation, limit, shards, heavy, kind=jnp.bfloat16):
    values = deviation * jax.random.normal(own_key, dims, jnp.float32)
    if shards:
        values = values * block_levels(own_key, dims, shards, -0.22, 0.18)
    return jnp.clip(spiked(values, jax.random.fold_in(own_key, 3), *heavy), -limit, limit).astype(kind)


def setup_inputs(seed: int = 0) -> dict:
    seeds = jax.random.split(jax.random.key(seed), 16)
    return {
        "tokens": bell_draw(seeds[0], (TOKENS, D), 1.0, 6.0, ((0, 32),)),
        "w_qkv": bell_draw(seeds[1], (D, 3 * D), D ** -0.5, 0.1875, ((0, 2), (1, 16))),
        "w_proj": bell_draw(seeds[2], (D, D), (max(1, D // LEN)) ** -0.5, 6.0, ((0, 2), (1, 16))),
        "w_fc1": bell_draw(seeds[3], (D, FF), D ** -0.5, 0.1875, ((0, 2), (1, 16))),
        "w_fc2": bell_draw(seeds[4], (FF, D), FF ** -0.5, 0.09375, ((0, 2), (1, 16))),
        "ln1_gain": jnp.clip(1.0 + 0.18 * jax.random.normal(seeds[5], (D,), jnp.float32), 0.099609375, 1.8984375).astype(jnp.bfloat16),
        "ln1_bias": bell_draw(seeds[6], (D,), 0.5, 6.0, ((0, 32),)),
        "q_bias": bell_draw(seeds[7], (D,), 0.5, 6.0, ((0, 32),)),
        "v_bias": bell_draw(seeds[8], (D,), 0.03, 0.4375, ((0, 32),)),
        "proj_bias": bell_draw(seeds[9], (D,), 0.5, 6.0, ((0, 32),)),
        "ln2_gain": jnp.clip(1.0 + 0.18 * jax.random.normal(seeds[10], (D,), jnp.float32), 0.099609375, 1.8984375).astype(jnp.bfloat16),
        "ln2_bias": bell_draw(seeds[11], (D,), 0.5, 6.0, ((0, 32),)),
        "fc1_bias": bell_draw(seeds[12], (FF,), 0.5, 6.0, ((0, 32),)),
        "fc2_bias": bell_draw(seeds[13], (D,), 0.5, 6.0, ((0, 32),)),
        "cotangent": noise_with(seeds[14], (TOKENS, D), 1.0, 6.0, ((0, 32),), (0, 1, 32, 2.75), jnp.float32),
    }


EPSILON = 1e-06

@jax.custom_vjp
def low(v):
    return lax.optimization_barrier(v.astype(jnp.bfloat16)).astype(jnp.float32)

@jax.custom_vjp
def low_back(v):
    return v

def low_keep(v):
    return (low(v), None)

def low_pass(kept, grad):
    return (grad,)

def back_keep(v):
    return (v, None)

def back_low(kept, grad):
    return (low(grad),)
low.defvjp(low_keep, low_pass)
low_back.defvjp(back_keep, back_low)

def layer_norm(value, gain, shift):
    average = lax.optimization_barrier(jnp.mean(value, axis=-1, keepdims=True))
    centred = value - average
    spread = lax.optimization_barrier(jnp.mean(centred * centred, axis=-1, keepdims=True))
    return centred * lax.rsqrt(spread + EPSILON) * gain + shift

def product(first, second):
    return jnp.dot(first, second, precision=lax.Precision.HIGHEST)

@jax.checkpoint
def attention_core(queries, key_rows, value_rows):
    scores = low_back(jnp.einsum('qhd,khd->hqk', queries, key_rows, precision=lax.Precision.HIGHEST) * HD ** (-0.5))
    weights_low = low(jax.nn.softmax(scores, axis=-1))
    return jnp.einsum('hqk,khd->qhd', weights_low, value_rows, precision=lax.Precision.HIGHEST)

def clip_layer(inputs, w_qkv, w_proj, w_fc1, w_fc2, ln1_gain, ln1_bias, q_bias, v_bias, proj_bias, ln2_gain, ln2_bias, fc1_bias, fc2_bias):
    hidden_one = low(layer_norm(inputs, ln1_gain, ln1_bias))
    qkv_bias = jnp.concatenate([q_bias, jnp.zeros_like(q_bias), v_bias])
    triple = low(low_back(product(hidden_one, w_qkv) + qkv_bias)).reshape(LEN, 3, H, HD)
    attended = attention_core(triple[:, 0], triple[:, 1], triple[:, 2]).reshape(LEN, D)
    attended = low(low_back(attended))
    middle = inputs + low_back(product(attended, w_proj) + proj_bias)
    hidden_two = low(layer_norm(middle, ln2_gain, ln2_bias))
    pre_act = low_back(product(hidden_two, w_fc1) + fc1_bias)
    activated = low(jax.nn.gelu(pre_act, approximate=False))
    return middle + low_back(product(activated, w_fc2) + fc2_bias)

def reference(tokens, w_qkv, w_proj, w_fc1, w_fc2, ln1_gain, ln1_bias, q_bias, v_bias, proj_bias, ln2_gain, ln2_bias, fc1_bias, fc2_bias, cotangent):
    params = tuple((value.astype(jnp.float32) for value in (w_qkv, w_proj, w_fc1, w_fc2, ln1_gain, ln1_bias, q_bias, v_bias, proj_bias, ln2_gain, ln2_bias, fc1_bias, fc2_bias)))
    clip_inputs = tokens.astype(jnp.float32).reshape(CLIPS, LEN, D)
    clip_cotangents = cotangent.astype(jnp.float32).reshape(CLIPS, LEN, D)

    def advance(summed, element):
        clip_input, clip_cotangent = element
        result, pullback = jax.vjp(clip_layer, clip_input, *params)
        gradients = pullback(clip_cotangent)
        summed = tuple((running + fresh for running, fresh in zip(summed, gradients[1:])))
        return (summed, (result.astype(jnp.bfloat16), gradients[0]))
    zeroes = tuple((jnp.zeros_like(value) for value in params))
    summed, (results, grad_inputs) = lax.scan(advance, zeroes, (clip_inputs, clip_cotangents))
    return (results.reshape(TOKENS, D), grad_inputs.reshape(TOKENS, D), summed[0], summed[1], summed[2], summed[3], summed[4], summed[5], summed[6], summed[7], summed[8], summed[9], summed[10], summed[11], summed[12])
```

```python
import math

import jax
import jax.numpy as jnp
from jax import lax
from jax.experimental import pallas as pl
from jax.experimental.pallas import tpu as pltpu
from jax.sharding import PartitionSpec as P

D = 1024
H = 16
HD = 64
LEN = 1568


EPSILON = 1e-06


def layer_norm(value, gain, shift):
    average = jnp.mean(value, axis=-1, keepdims=True)
    centred = value - average
    spread = jnp.mean(centred * centred, axis=-1, keepdims=True)
    inverse = lax.rsqrt(spread + EPSILON)
    normed = centred * inverse
    return (normed * gain + shift, normed, inverse)


def norm_back(grad_out, normed, inverse, gain):
    scaled = grad_out * gain
    mean_first = jnp.mean(scaled, axis=-1, keepdims=True)
    mean_second = jnp.mean(scaled * normed, axis=-1, keepdims=True)
    return inverse * (scaled - mean_first - normed * mean_second)


def gelu_slope(pre_act):
    cumulative = 0.5 * (1.0 + lax.erf(pre_act * 2.0 ** (-0.5)))
    density = jnp.exp(-0.5 * pre_act * pre_act) * (2.0 * math.pi) ** (-0.5)
    return cumulative + pre_act * density


def inner_rows(first, second):
    return lax.dot_general(
        first, second, (((0,), (0,)), ((), ())), preferred_element_type=jnp.float32
    )


def outer_cols(first, second):
    return lax.dot_general(
        first, second, (((1,), (1,)), ((), ())), preferred_element_type=jnp.float32
    )


def clip_forward(block):
    queries, key_rows, value_rows = (block[:, 0], block[:, 1], block[:, 2])
    scores = jnp.einsum(
        "qhd,khd->hqk", queries, key_rows, preferred_element_type=jnp.float32
    ) * HD ** (-0.5)
    row_peak = jnp.max(scores, axis=-1, keepdims=True)
    exponent = jnp.exp(scores - row_peak)
    row_total = jnp.sum(exponent, axis=-1, keepdims=True)
    weights_low = (exponent / row_total).astype(jnp.bfloat16)
    mixed_heads = jnp.einsum(
        "hqk,khd->qhd", weights_low, value_rows, preferred_element_type=jnp.float32
    )
    return (mixed_heads.astype(jnp.bfloat16), (row_peak + jnp.log(row_total))[..., 0])


def clip_backward(element):
    block, grad_mixed, logsum = element
    queries, key_rows, value_rows = (block[:, 0], block[:, 1], block[:, 2])
    scores = jnp.einsum(
        "qhd,khd->hqk", queries, key_rows, preferred_element_type=jnp.float32
    ) * HD ** (-0.5)
    weights_full = jnp.exp(scores - logsum[..., None])
    weights_low = weights_full.astype(jnp.bfloat16)
    grad_values = jnp.einsum(
        "hqk,qhd->khd", weights_low, grad_mixed, preferred_element_type=jnp.float32
    )
    grad_weights = jnp.einsum(
        "qhd,khd->hqk", grad_mixed, value_rows, preferred_element_type=jnp.float32
    )
    row_delta = jnp.sum(grad_weights * weights_full, axis=-1, keepdims=True)
    grad_scores = (weights_full * (grad_weights - row_delta)).astype(jnp.bfloat16)
    grad_queries = jnp.einsum(
        "hqk,khd->qhd", grad_scores, key_rows, preferred_element_type=jnp.float32
    ) * HD ** (-0.5)
    grad_keys = jnp.einsum(
        "hqk,qhd->khd", grad_scores, queries, preferred_element_type=jnp.float32
    ) * HD ** (-0.5)
    return jnp.stack([grad_queries, grad_keys, grad_values], axis=1).astype(jnp.bfloat16)


def per_device(
    tokens,
    w_qkv,
    w_proj,
    w_fc1,
    w_fc2,
    ln1_gain,
    ln1_bias,
    q_bias,
    v_bias,
    proj_bias,
    ln2_gain,
    ln2_bias,
    fc1_bias,
    fc2_bias,
    cotangent,
):
    (
        qkv_part,
        proj_part,
        fc1_part,
        fc2_part,
        gain1_part,
        shift1_part,
        biasq_part,
        biasv_part,
        biasp_part,
        gain2_part,
        shift2_part,
        bias1_part,
        bias2_part,
    ) = (
        lax.all_gather(w_qkv, "row", axis=0, tiled=True),
        lax.all_gather(w_proj, "row", axis=0, tiled=True),
        lax.all_gather(w_fc1, "row", axis=0, tiled=True),
        lax.all_gather(w_fc2, "row", axis=0, tiled=True),
        lax.all_gather(ln1_gain, "row", axis=0, tiled=True),
        lax.all_gather(ln1_bias, "row", axis=0, tiled=True),
        lax.all_gather(q_bias, "row", axis=0, tiled=True),
        lax.all_gather(v_bias, "row", axis=0, tiled=True),
        lax.all_gather(proj_bias, "row", axis=0, tiled=True),
        lax.all_gather(ln2_gain, "row", axis=0, tiled=True),
        lax.all_gather(ln2_bias, "row", axis=0, tiled=True),
        lax.all_gather(fc1_bias, "row", axis=0, tiled=True),
        lax.all_gather(fc2_bias, "row", axis=0, tiled=True),
    )
    (
        full_qkv,
        full_proj,
        full_fc1,
        full_fc2,
        full_gain1,
        full_shift1,
        full_biasq,
        full_biasv,
        full_biasp,
        full_gain2,
        full_shift2,
        full_bias1,
        full_bias2,
    ) = (
        lax.all_gather(qkv_part, "col", axis=1, tiled=True),
        lax.all_gather(proj_part, "col", axis=1, tiled=True),
        lax.all_gather(fc1_part, "col", axis=1, tiled=True),
        lax.all_gather(fc2_part, "col", axis=1, tiled=True),
        lax.all_gather(gain1_part, "col", axis=0, tiled=True),
        lax.all_gather(shift1_part, "col", axis=0, tiled=True),
        lax.all_gather(biasq_part, "col", axis=0, tiled=True),
        lax.all_gather(biasv_part, "col", axis=0, tiled=True),
        lax.all_gather(biasp_part, "col", axis=0, tiled=True),
        lax.all_gather(gain2_part, "col", axis=0, tiled=True),
        lax.all_gather(shift2_part, "col", axis=0, tiled=True),
        lax.all_gather(bias1_part, "col", axis=0, tiled=True),
        lax.all_gather(bias2_part, "col", axis=0, tiled=True),
    )
    gain_first = full_gain1.astype(jnp.float32)
    gain_second = full_gain2.astype(jnp.float32)
    groups = lax.axis_size("row")
    heads_local = H // groups
    per_group = heads_local * HD
    inputs = tokens.astype(jnp.float32)
    token_rows = inputs.shape[0]
    normed_out1, normed_one, inverse_one = layer_norm(
        inputs, gain_first, full_shift1.astype(jnp.float32)
    )
    hidden_one = normed_out1.astype(jnp.bfloat16)
    bias_q = full_biasq.astype(jnp.float32)
    qkv_bias = jnp.concatenate([bias_q, jnp.zeros_like(bias_q), full_biasv.astype(jnp.float32)])
    projected = jnp.dot(hidden_one, full_qkv, preferred_element_type=jnp.float32) + qkv_bias
    qkv_low = projected.astype(jnp.bfloat16).reshape(token_rows, 3, groups, per_group)
    by_heads = lax.all_to_all(qkv_low, "row", split_axis=2, concat_axis=0, tiled=True)
    col_rows = by_heads.shape[0]
    clip_count = col_rows // LEN
    blocks = by_heads.reshape(clip_count, LEN, 3, heads_local, HD)
    mixed_heads, logsum = lax.map(clip_forward, blocks)
    attended = lax.all_to_all(
        mixed_heads.reshape(col_rows, 1, per_group), "row", split_axis=0, concat_axis=1, tiled=True
    ).reshape(token_rows, D)
    middle = inputs + (
        jnp.dot(attended, full_proj, preferred_element_type=jnp.float32)
        + full_biasp.astype(jnp.float32)
    )
    normed_out2, normed_two, inverse_two = layer_norm(
        middle, gain_second, full_shift2.astype(jnp.float32)
    )
    hidden_two = normed_out2.astype(jnp.bfloat16)
    pre_act = jnp.dot(hidden_two, full_fc1, preferred_element_type=jnp.float32) + full_bias1.astype(
        jnp.float32
    )
    activated = jax.nn.gelu(pre_act, approximate=False).astype(jnp.bfloat16)
    result = middle + (
        jnp.dot(activated, full_fc2, preferred_element_type=jnp.float32)
        + full_bias2.astype(jnp.float32)
    )
    qkv_again, proj_again, fc1_again, fc2_again = (
        lax.all_gather(w_qkv, "row", axis=0, tiled=True),
        lax.all_gather(w_proj, "row", axis=0, tiled=True),
        lax.all_gather(w_fc1, "row", axis=0, tiled=True),
        lax.all_gather(w_fc2, "row", axis=0, tiled=True),
    )
    back_qkv, back_proj, back_fc1, back_fc2 = (
        lax.all_gather(qkv_again, "col", axis=1, tiled=True),
        lax.all_gather(proj_again, "col", axis=1, tiled=True),
        lax.all_gather(fc1_again, "col", axis=1, tiled=True),
        lax.all_gather(fc2_again, "col", axis=1, tiled=True),
    )
    grad_out = cotangent.astype(jnp.bfloat16)
    grad_bias2 = jnp.sum(grad_out.astype(jnp.float32), axis=0)
    grad_fc2 = inner_rows(activated, grad_out)
    grad_act = outer_cols(grad_out, back_fc2)
    grad_pre = (grad_act * gelu_slope(pre_act)).astype(jnp.bfloat16)
    grad_bias1 = jnp.sum(grad_pre.astype(jnp.float32), axis=0)
    grad_fc1 = inner_rows(hidden_two, grad_pre)
    grad_hidden2 = outer_cols(grad_pre, back_fc1)
    grad_gain2 = jnp.sum(grad_hidden2 * normed_two, axis=0)
    grad_shift2 = jnp.sum(grad_hidden2, axis=0)
    grad_middle = cotangent + norm_back(grad_hidden2, normed_two, inverse_two, gain_second)
    grad_branch = grad_middle.astype(jnp.bfloat16)
    grad_biasp = jnp.sum(grad_branch.astype(jnp.float32), axis=0)
    grad_proj = inner_rows(attended, grad_branch)
    grad_attended = outer_cols(grad_branch, back_proj).astype(jnp.bfloat16)
    grad_heads = lax.all_to_all(
        grad_attended.reshape(token_rows, groups, per_group),
        "row",
        split_axis=1,
        concat_axis=0,
        tiled=True,
    )
    grad_blocks = grad_heads.reshape(clip_count, LEN, heads_local, HD)
    grad_triple = lax.map(clip_backward, (blocks, grad_blocks, logsum))
    grad_tokens_qkv = lax.all_to_all(
        grad_triple.reshape(col_rows, 3, 1, per_group),
        "row",
        split_axis=0,
        concat_axis=2,
        tiled=True,
    ).reshape(token_rows, 3 * D)
    grad_qkv_float = grad_tokens_qkv.astype(jnp.float32)
    grad_biasq = jnp.sum(grad_qkv_float[:, :D], axis=0)
    grad_biasv = jnp.sum(grad_qkv_float[:, 2 * D :], axis=0)
    grad_qkv = inner_rows(hidden_one, grad_tokens_qkv)
    grad_hidden1 = outer_cols(grad_tokens_qkv, back_qkv)
    grad_gain1 = jnp.sum(grad_hidden1 * normed_one, axis=0)
    grad_shift1 = jnp.sum(grad_hidden1, axis=0)
    grad_inputs = grad_middle + norm_back(grad_hidden1, normed_one, inverse_one, gain_first)
    (
        sum_qkv,
        sum_proj,
        sum_fc1,
        sum_fc2,
        sum_gain1,
        sum_shift1,
        sum_biasq,
        sum_biasv,
        sum_biasp,
        sum_gain2,
        sum_shift2,
        sum_bias1,
        sum_bias2,
    ) = (
        lax.psum_scatter(
            grad_qkv.astype(jnp.bfloat16), "col", scatter_dimension=1, tiled=True
        ).astype(jnp.float32),
        lax.psum_scatter(
            grad_proj.astype(jnp.bfloat16), "col", scatter_dimension=1, tiled=True
        ).astype(jnp.float32),
        lax.psum_scatter(
            grad_fc1.astype(jnp.bfloat16), "col", scatter_dimension=1, tiled=True
        ).astype(jnp.float32),
        lax.psum_scatter(
            grad_fc2.astype(jnp.bfloat16), "col", scatter_dimension=1, tiled=True
        ).astype(jnp.float32),
        lax.psum_scatter(
            grad_gain1.astype(jnp.bfloat16), "col", scatter_dimension=0, tiled=True
        ).astype(jnp.float32),
        lax.psum_scatter(
            grad_shift1.astype(jnp.bfloat16), "col", scatter_dimension=0, tiled=True
        ).astype(jnp.float32),
        lax.psum_scatter(
            grad_biasq.astype(jnp.bfloat16), "col", scatter_dimension=0, tiled=True
        ).astype(jnp.float32),
        lax.psum_scatter(
            grad_biasv.astype(jnp.bfloat16), "col", scatter_dimension=0, tiled=True
        ).astype(jnp.float32),
        lax.psum_scatter(
            grad_biasp.astype(jnp.bfloat16), "col", scatter_dimension=0, tiled=True
        ).astype(jnp.float32),
        lax.psum_scatter(
            grad_gain2.astype(jnp.bfloat16), "col", scatter_dimension=0, tiled=True
        ).astype(jnp.float32),
        lax.psum_scatter(
            grad_shift2.astype(jnp.bfloat16), "col", scatter_dimension=0, tiled=True
        ).astype(jnp.float32),
        lax.psum_scatter(
            grad_bias1.astype(jnp.bfloat16), "col", scatter_dimension=0, tiled=True
        ).astype(jnp.float32),
        lax.psum_scatter(
            grad_bias2.astype(jnp.bfloat16), "col", scatter_dimension=0, tiled=True
        ).astype(jnp.float32),
    )
    (
        out_qkv,
        out_proj,
        out_fc1,
        out_fc2,
        out_gain1,
        out_shift1,
        out_biasq,
        out_biasv,
        out_biasp,
        out_gain2,
        out_shift2,
        out_bias1,
        out_bias2,
    ) = (
        lax.psum_scatter(
            sum_qkv.astype(jnp.bfloat16), "row", scatter_dimension=0, tiled=True
        ).astype(jnp.float32),
        lax.psum_scatter(
            sum_proj.astype(jnp.bfloat16), "row", scatter_dimension=0, tiled=True
        ).astype(jnp.float32),
        lax.psum_scatter(
            sum_fc1.astype(jnp.bfloat16), "row", scatter_dimension=0, tiled=True
        ).astype(jnp.float32),
        lax.psum_scatter(
            sum_fc2.astype(jnp.bfloat16), "row", scatter_dimension=0, tiled=True
        ).astype(jnp.float32),
        lax.psum_scatter(
            sum_gain1.astype(jnp.bfloat16), "row", scatter_dimension=0, tiled=True
        ).astype(jnp.float32),
        lax.psum_scatter(
            sum_shift1.astype(jnp.bfloat16), "row", scatter_dimension=0, tiled=True
        ).astype(jnp.float32),
        lax.psum_scatter(
            sum_biasq.astype(jnp.bfloat16), "row", scatter_dimension=0, tiled=True
        ).astype(jnp.float32),
        lax.psum_scatter(
            sum_biasv.astype(jnp.bfloat16), "row", scatter_dimension=0, tiled=True
        ).astype(jnp.float32),
        lax.psum_scatter(
            sum_biasp.astype(jnp.bfloat16), "row", scatter_dimension=0, tiled=True
        ).astype(jnp.float32),
        lax.psum_scatter(
            sum_gain2.astype(jnp.bfloat16), "row", scatter_dimension=0, tiled=True
        ).astype(jnp.float32),
        lax.psum_scatter(
            sum_shift2.astype(jnp.bfloat16), "row", scatter_dimension=0, tiled=True
        ).astype(jnp.float32),
        lax.psum_scatter(
            sum_bias1.astype(jnp.bfloat16), "row", scatter_dimension=0, tiled=True
        ).astype(jnp.float32),
        lax.psum_scatter(
            sum_bias2.astype(jnp.bfloat16), "row", scatter_dimension=0, tiled=True
        ).astype(jnp.float32),
    )
    return (
        result.astype(jnp.bfloat16),
        grad_inputs,
        out_qkv,
        out_proj,
        out_fc1,
        out_fc2,
        out_gain1,
        out_shift1,
        out_biasq,
        out_biasv,
        out_biasp,
        out_gain2,
        out_shift2,
        out_bias1,
        out_bias2,
    )


bf16 = jnp.bfloat16
f32 = jnp.float32
FF = 4096
ROWS_QKV, ROWS_A = 768, 784
ROWS_FC, ROWS_PROJ, ROWS_B = 1024, 256, 2304
VMEM_LIMIT = 62 * 1024 * 1024
NT = (((1,), (1,)), ((), ()))
TN = (((0,), (0,)), ((), ()))


def params(limit=VMEM_LIMIT):
    return pltpu.CompilerParams(vmem_limit_bytes=limit)


def cost(flops, data, trans=0):
    return pl.CostEstimate(flops=int(flops), bytes_accessed=int(data), transcendentals=int(trans))


def once(shape, index):
    return pl.BlockSpec(shape, index, pipeline_mode=pl.Buffered(1))


def halves_cat(first, second):
    return jnp.concatenate([first[:, :64], second[:, :64]], axis=1)


def row_stats(value):
    average = jnp.mean(value, axis=-1, keepdims=True)
    centred = value - average
    spread = jnp.mean(centred * centred, axis=-1, keepdims=True)
    inverse = lax.rsqrt(spread + EPSILON)
    return centred * inverse, inverse


def pack_qkv(block):
    tail = block[:, 128:]
    return jnp.concatenate(
        [block[:, :128], jnp.concatenate([tail[:256], tail[256:]], axis=1)], axis=0
    )


def unpack_qkv(rows):
    tail = rows[512:768]
    return jnp.concatenate(
        [rows[:512], jnp.concatenate([tail[:, :64], tail[:, 64:]], axis=0)], axis=1
    )


def pack_proj(block):
    return jnp.concatenate([block[:256], block[256:]], axis=1)


def unpack_proj(rows):
    return jnp.concatenate([rows[:, :64], rows[:, 64:]], axis=0)


def pack_fc1(block):
    return jnp.concatenate([block[:, :128], block[:, 128:]], axis=0)


def unpack_fc1(rows):
    return jnp.concatenate([rows[:512], rows[512:]], axis=1)


def pack_fc2(block):
    return block.reshape(4, 2, 256, 64).transpose(0, 2, 1, 3).reshape(1024, 128)


def unpack_fc2(rows):
    return rows.reshape(4, 256, 2, 64).transpose(0, 2, 1, 3).reshape(2048, 64)


def assemble_qkv(w_refs, w_out):
    for r in range(2):
        w0, w1 = w_refs[r][0][0], w_refs[r][1][0]
        a0, b0 = w0[:512], w0[512:768]
        a1, b1 = w1[:512], w1[512:768]
        lo = slice(512 * r, 512 * r + 256)
        hi = slice(512 * r + 256, 512 * r + 512)
        w_out[512 * r : 512 * r + 512, 0:128] = a0
        w_out[lo, 128:256] = jnp.concatenate([b0[:, :64], a1[:256, :64]], axis=1)
        w_out[hi, 128:256] = jnp.concatenate([b0[:, 64:], a1[256:, :64]], axis=1)
        w_out[lo, 256:384] = jnp.concatenate([a1[:256, 64:], b1[:, :64]], axis=1)
        w_out[hi, 256:384] = jnp.concatenate([a1[256:, 64:], b1[:, 64:]], axis=1)


def qkv_body(tok, x_own, x_oth, w00, w01, w10, w11, gain, shift, bias, h_ref, qkv_ref, w_sc):
    step = pl.program_id(0)

    @pl.when(step == 0)
    def _():
        for half, x_ref in enumerate((x_own, x_oth)):
            for i in range(tok // 112):
                rows = x_ref[i * 112 : (i + 1) * 112, :].astype(f32)
                normed, _ = row_stats(rows)
                h_ref[half * tok + i * 112 : half * tok + (i + 1) * 112, :] = (
                    normed * gain[...] + shift[...]
                ).astype(bf16)

    assemble_qkv(((w00, w01), (w10, w11)), w_sc)

    def project(rows):
        out = jnp.dot(h_ref[0:rows, :], w_sc[...], preferred_element_type=f32) + bias[...]
        out = out.astype(bf16)
        for i in range(3):
            tile = 3 * step + i
            part, column = tile // 8, tile % 8
            qkv_ref[part, 0:rows, pl.ds(pl.multiple_of(column * 128, 128), 128)] = out[
                :, i * 128 : (i + 1) * 128
            ]

    @pl.when(step < 2)
    def _():
        project(tok)

    @pl.when(step >= 2)
    def _():
        project(2 * tok)


def qkv_call(x_own, x_oth, table, gathered, gain, shift, bias):
    tok = x_own.shape[0]

    def weight(r, k):
        return pl.BlockSpec((1, ROWS_A, 128), lambda j, t: (t[r * 16 + 2 * j + k], 0, 0))

    return pl.pallas_call(
        lambda t, *refs: qkv_body(tok, *refs),
        out_shape=(
            jax.ShapeDtypeStruct((2 * tok, D), bf16),
            jax.ShapeDtypeStruct((3, 2 * tok, D), bf16),
        ),
        grid_spec=pltpu.PrefetchScalarGridSpec(
            num_scalar_prefetch=1,
            grid=(8,),
            in_specs=[
                once((tok, D), lambda j, t: (0, 0)),
                once((tok, D), lambda j, t: (0, 0)),
                weight(0, 0),
                weight(0, 1),
                weight(1, 0),
                weight(1, 1),
                once((1, D), lambda j, t: (0, 0)),
                once((1, D), lambda j, t: (0, 0)),
                pl.BlockSpec((1, 384), lambda j, t: (0, j)),
            ],
            out_specs=[
                once((2 * tok, D), lambda j, t: (0, 0)),
                once((3, 2 * tok, D), lambda j, t: (0, 0, 0)),
            ],
            scratch_shapes=[pltpu.VMEM((D, 384), bf16)],
        ),
        compiler_params=params(),
        cost_estimate=cost(2 * tok * D * D * 5, 24e6),
        name="qkv_forward",
    )(table, x_own, x_oth, gathered, gathered, gathered, gathered, gain, shift, bias)


def attend_body(tok, keys, chunk, q_ref, k_ref, v_ref, o_ref, l_ref, *scratch):
    vt_a, vt_b, qm, s_a, s_b, m_a, m_b, acc_sc, o_sc = scratch
    count = keys // chunk
    lane = lax.broadcasted_iota(jnp.int32, (1, 128), 1)
    q2 = q_ref[...] * jnp.asarray(HD**-0.5, bf16)
    zero = jnp.zeros_like(q2)

    def stage(q_head, s_w, m_w, s_r, m_r, vt_r):
        peak = jnp.max(m_r[...], axis=0, keepdims=True)
        acc_sc[...] = jnp.zeros_like(acc_sc)
        qm[...] = q_head
        m_w[...] = jnp.full_like(m_w, -jnp.inf)
        for i in range(count):
            rows = slice(i * chunk, (i + 1) * chunk)
            s = lax.dot_general(k_ref[rows, :], qm[...], NT, preferred_element_type=f32)
            s_w[rows, :] = s
            m_w[...] = jnp.maximum(m_w[...], jnp.max(s.reshape(chunk // 8, 8, tok), axis=0))
            p = jnp.exp(s_r[rows, :] - peak).astype(bf16)
            acc_sc[...] += jnp.dot(vt_r[i], p, preferred_element_type=f32)
        acc = acc_sc[...]
        total = acc[64:65]
        return acc[0:64] * (1.0 / total), peak + jnp.log(total)

    out_b, lse_b = stage(jnp.where(lane < 64, q2, zero), s_a, m_a, s_b, m_b, vt_b)
    o_ref[0:64] = o_sc[0:64].astype(bf16)
    o_ref[64:128] = out_b.astype(bf16)
    l_ref[0] = o_sc[64:65]
    l_ref[1] = lse_b
    ones = jnp.ones((16, chunk), bf16)
    for i in range(count):
        vt = v_ref[i * chunk : (i + 1) * chunk, :].T
        vt_a[i, 0:64] = vt[0:64]
        vt_a[i, 64:80] = ones
        vt_b[i, 0:64] = vt[64:128]
        vt_b[i, 64:80] = ones
    out_a, lse_a = stage(jnp.where(lane < 64, zero, q2), s_b, m_b, s_a, m_a, vt_a)
    o_sc[0:64] = out_a
    o_sc[64:65] = lse_a


def attend_call(qkv, tok, chunk=224):
    keys = qkv.shape[1]
    pairs = H // 2

    def column(part, rows):
        return pl.BlockSpec((None, rows, 128), lambda g: (part, 0, jnp.minimum(g, pairs - 1)))

    def behind(g):
        return jnp.maximum(g - 1, 0)

    return pl.pallas_call(
        lambda *refs: attend_body(tok, keys, chunk, *refs),
        out_shape=(
            jax.ShapeDtypeStruct((D, tok), bf16),
            jax.ShapeDtypeStruct((H, 1, tok), f32),
        ),
        grid=(pairs + 1,),
        in_specs=[column(0, tok), column(1, keys), column(2, keys)],
        out_specs=[
            pl.BlockSpec((128, tok), lambda g: (behind(g), 0)),
            pl.BlockSpec((2, 1, tok), lambda g: (behind(g), 0, 0)),
        ],
        scratch_shapes=[
            pltpu.VMEM((keys // chunk, 80, chunk), bf16),
            pltpu.VMEM((keys // chunk, 80, chunk), bf16),
            pltpu.VMEM((tok, 128), bf16),
            pltpu.VMEM((keys, tok), f32),
            pltpu.VMEM((keys, tok), f32),
            pltpu.VMEM((8, tok), f32),
            pltpu.VMEM((8, tok), f32),
            pltpu.VMEM((80, tok), f32),
            pltpu.VMEM((72, tok), f32),
        ],
        compiler_params=params(),
        cost_estimate=cost(16 * 4 * tok * keys * 256, 12e6, 16 * tok * keys),
        name="attention_forward",
    )(qkv, qkv, qkv)


def attend_back_body(tok, keys, chunk, q_ref, k_ref, v_ref, g_ref, o_ref, l_ref, out_ref, *scratch):
    qx, gx, q_t, g_t, dq_sc = scratch
    lane = lax.broadcasted_iota(jnp.int32, (1, 128), 1)
    row = lax.broadcasted_iota(jnp.int32, (128, 1), 0)
    q2 = q_ref[...] * jnp.asarray(HD**-0.5, bf16)
    grad = g_ref[...]
    qx[:, 0:128] = q2
    gx[:, 0:128] = grad
    q_t[...] = q2.T
    g_t[...] = grad.T
    prod = g_t[...].astype(f32) * o_ref[...].astype(f32)

    def split(value):
        terms, rest = [], value
        for _ in range(3):
            term = rest.astype(bf16).astype(f32)
            terms.append(term)
            rest = rest - term
        return terms

    s_col = jnp.zeros((128, tok), f32)
    d_col = jnp.zeros((128, tok), f32)
    for h in range(2):
        delta = jnp.sum(prod[h * 64 : h * 64 + 64], axis=0, keepdims=True)
        for t, (a, b) in enumerate(zip(split(-l_ref[h]), split(-delta))):
            s_col = jnp.where(row == h * 4 + t, a, s_col)
            d_col = jnp.where(row == h * 4 + t, b, d_col)
    qx[:, 128:256] = s_col.astype(bf16).T
    gx[:, 128:256] = d_col.astype(bf16).T
    dq_sc[...] = jnp.zeros_like(dq_sc)
    for i in range(keys // chunk):
        rows = slice(i * chunk, (i + 1) * chunk)
        ks, vs = k_ref[rows, :], v_ref[rows, :]
        dvs, dks, dq = [], [], None
        for h in range(2):
            mine = (lane >= h * 64) & (lane < h * 64 + 64)
            pick = jnp.broadcast_to(
                ((lane >= h * 4) & (lane < h * 4 + 3)).astype(bf16), (chunk, 128)
            )
            km = jnp.where(mine, ks, jnp.zeros_like(ks))
            vm = jnp.where(mine, vs, jnp.zeros_like(vs))
            p = jnp.exp(
                lax.dot_general(
                    qx[...], jnp.concatenate([km, pick], 1), NT, preferred_element_type=f32
                )
            )
            dp = lax.dot_general(
                gx[...], jnp.concatenate([vm, pick], 1), NT, preferred_element_type=f32
            )
            ds = (p * dp).astype(bf16)
            p_low = p.astype(bf16)
            head = slice(h * 64, h * 64 + 64)
            dvs.append(jnp.dot(g_t[head], p_low, preferred_element_type=f32))
            dks.append(jnp.dot(q_t[head], ds, preferred_element_type=f32))
            part = jnp.dot(ds, km, preferred_element_type=f32)
            dq = part if dq is None else dq + part
        dq_sc[...] += dq
        out_ref[1, rows, :] = jnp.concatenate(dks, 0).T.astype(bf16)
        out_ref[2, rows, :] = jnp.concatenate(dvs, 0).T.astype(bf16)
    out_ref[0, 0:tok, :] = (dq_sc[...] * HD**-0.5).astype(bf16)
    out_ref[0, tok:keys, :] = jnp.zeros((keys - tok, 128), bf16)


def attend_back_call(qkv, grad, mixed, logsum, chunk=224):
    tok = grad.shape[0]
    keys = qkv.shape[1]

    def column(part, rows):
        return pl.BlockSpec((None, rows, 128), lambda g: (part, 0, g))

    return pl.pallas_call(
        lambda *refs: attend_back_body(tok, keys, chunk, *refs),
        out_shape=jax.ShapeDtypeStruct((3, keys, D), bf16),
        grid=(H // 2,),
        in_specs=[
            column(0, tok),
            column(1, keys),
            column(2, keys),
            pl.BlockSpec((tok, 128), lambda g: (0, g)),
            pl.BlockSpec((128, tok), lambda g: (g, 0)),
            pl.BlockSpec((2, 1, tok), lambda g: (g, 0, 0)),
        ],
        out_specs=pl.BlockSpec((3, keys, 128), lambda g: (0, 0, g)),
        scratch_shapes=[
            pltpu.VMEM((tok, 256), bf16),
            pltpu.VMEM((tok, 256), bf16),
            pltpu.VMEM((128, tok), bf16),
            pltpu.VMEM((128, tok), bf16),
            pltpu.VMEM((tok, 128), f32),
        ],
        compiler_params=params(),
        cost_estimate=cost(16 * 8 * tok * keys * 256, 24e6, 16 * tok * keys),
        name="attention_backward",
    )(qkv, qkv, qkv, grad, mixed, logsum)


def gelu_parts(value):
    size = jnp.abs(value)
    bell = jnp.exp(-0.5 * value * value)
    t = 1.0 / (1.0 + (0.3275911 * 2.0**-0.5) * size)
    poly = t * (
        0.254829592
        + t * (-0.284496736 + t * (1.421413741 + t * (-1.453152027 + t * 1.061405429)))
    )
    upper = 0.5 * poly * bell
    phi = jnp.where(value >= 0.0, 1.0 - upper, upper)
    return value * phi, phi + value * (bell * (2.0 * math.pi) ** -0.5)


def feed_body(
    tok, o_ref, x_ref, cot_ref, wp_ref, w1_ref, w2_ref, b1_ref, vec_ref,
    out_ref, dmid_ref, datt_ref, gp_ref, g1_ref, g2_ref, gb1_ref, gvec_ref,
    mid, h2, dm, y_acc, w1, w2, wp,
):
    step = pl.program_id(0)
    last = pl.num_programs(0) - 1
    part = 112
    pieces = [slice(i * part, (i + 1) * part) for i in range(tok // part)]

    @pl.when(step == 0)
    def _():
        for r in range(2):
            for c in range(8):
                p0, p1 = wp_ref[r * 16 + 2 * c], wp_ref[r * 16 + 2 * c + 1]
                cols = slice(128 * c, 128 * c + 128)
                wp[512 * r : 512 * r + 256, cols] = jnp.concatenate([p0[:, :64], p1[:, :64]], 1)
                wp[512 * r + 256 : 512 * r + 512, cols] = jnp.concatenate([p0[:, 64:], p1[:, 64:]], 1)
        mid[...] = lax.dot_general(o_ref[...], wp[...], TN, preferred_element_type=f32)
        for rows in pieces:
            total = x_ref[rows, :].astype(f32) + (mid[rows, :] + vec_ref[0:1, :])
            mid[rows, :] = total
            normed, _ = row_stats(total)
            h2[rows, :] = (normed * vec_ref[1:2, :] + vec_ref[2:3, :]).astype(bf16)
            dm[rows, :] = cot_ref[rows, :].astype(bf16)

    for r in range(2):
        for k in range(2):
            for s in range(2):
                w1[512 * r : 512 * r + 512, 256 * k + 128 * s : 256 * k + 128 * s + 128] = w1_ref[
                    r, k, 512 * s : 512 * s + 512, :
                ]
    for c in range(8):
        p0, p1 = w2_ref[0, 2 * c], w2_ref[0, 2 * c + 1]
        cols = slice(128 * c, 128 * c + 128)
        w2[0:256, cols] = jnp.concatenate([p0[:, :64], p1[:, :64]], 1)
        w2[256:512, cols] = jnp.concatenate([p0[:, 64:], p1[:, 64:]], 1)

    pre = jnp.dot(h2[...], w1[...], preferred_element_type=f32) + b1_ref[...]
    act, slope = gelu_parts(pre)
    act = act.astype(bf16)
    dact = lax.dot_general(dm[...], w2[...], NT, preferred_element_type=f32)
    dpre32 = dact * slope
    dpre = dpre32.astype(bf16)
    gb1_ref[...] = jnp.sum(dpre.astype(f32), axis=0, keepdims=True)
    y = jnp.dot(act, w2[...], preferred_element_type=f32)
    dh = lax.dot_general(dpre, w1[...], NT, preferred_element_type=f32)

    @pl.when(step == 0)
    def _():
        y_acc[...] = y
        dmid_ref[...] = dh

    @pl.when(step > 0)
    def _():
        y_acc[...] += y
        dmid_ref[...] += dh

    g1 = lax.dot_general(h2[...], dpre, TN, preferred_element_type=f32).astype(bf16)
    for r in range(2):
        for k in range(2):
            for s in range(2):
                g1_ref[r, k, 512 * s : 512 * s + 512, :] = g1[
                    512 * r : 512 * r + 512, 256 * k + 128 * s : 256 * k + 128 * s + 128
                ]
    g2 = lax.dot_general(act, dm[...], TN, preferred_element_type=f32).astype(bf16)
    for c in range(8):
        top = g2[0:256, 128 * c : 128 * c + 128]
        low = g2[256:512, 128 * c : 128 * c + 128]
        g2_ref[0, 2 * c] = jnp.concatenate([top[:, :64], low[:, :64]], 1)
        g2_ref[0, 2 * c + 1] = jnp.concatenate([top[:, 64:], low[:, 64:]], 1)

    @pl.when(step == last)
    def _():
        gain2 = vec_ref[1:2, :]
        sums = [jnp.zeros((1, D), f32) for _ in range(4)]
        for rows in pieces:
            out_ref[rows, :] = (mid[rows, :] + (y_acc[rows, :] + vec_ref[3:4, :])).astype(bf16)
            normed, inverse = row_stats(mid[rows, :])
            e = dmid_ref[rows, :]
            scaled = e * gain2
            first = jnp.mean(scaled, axis=-1, keepdims=True)
            second = jnp.mean(scaled * normed, axis=-1, keepdims=True)
            grad = cot_ref[rows, :] + inverse * (scaled - first - normed * second)
            dmid_ref[rows, :] = grad
            branch = grad.astype(bf16)
            h2[rows, :] = branch
            for i, term in enumerate((e * normed, e, branch.astype(f32), dm[rows, :].astype(f32))):
                sums[i] = sums[i] + jnp.sum(term, axis=0, keepdims=True)
        gvec_ref[...] = jnp.concatenate(sums + [jnp.zeros((4, D), f32)], 0)
        datt_ref[...] = lax.dot_general(h2[...], wp[...], NT, preferred_element_type=f32).astype(bf16)
        gp = jnp.dot(o_ref[...], h2[...], preferred_element_type=f32).astype(bf16)
        for r in range(2):
            for c in range(8):
                top = gp[512 * r : 512 * r + 256, 128 * c : 128 * c + 128]
                low = gp[512 * r + 256 : 512 * r + 512, 128 * c : 128 * c + 128]
                gp_ref[r * 16 + 2 * c] = jnp.concatenate([top[:, :64], low[:, :64]], 1)
                gp_ref[r * 16 + 2 * c + 1] = jnp.concatenate([top[:, 64:], low[:, 64:]], 1)


def feed_call(mixed, x_own, cot, gathered, bias1, vectors):
    tok = x_own.shape[0]
    by_block = gathered.reshape(2, 16, ROWS_B, 128)
    zero2 = lambda j: (0, 0)
    return pl.pallas_call(
        lambda *refs: feed_body(tok, *refs),
        out_shape=(
            jax.ShapeDtypeStruct((tok, D), bf16),
            jax.ShapeDtypeStruct((tok, D), f32),
            jax.ShapeDtypeStruct((tok, D), bf16),
            jax.ShapeDtypeStruct((32, ROWS_PROJ, 128), bf16),
            jax.ShapeDtypeStruct((2, 16, ROWS_FC, 128), bf16),
            jax.ShapeDtypeStruct((2, 16, ROWS_FC, 128), bf16),
            jax.ShapeDtypeStruct((1, FF), f32),
            jax.ShapeDtypeStruct((8, D), f32),
        ),
        grid=(8,),
        in_specs=[
            once((D, tok), zero2),
            once((tok, D), zero2),
            once((tok, D), zero2),
            once((32, ROWS_PROJ, 128), lambda j: (0, 8, 0)),
            pl.BlockSpec((2, 2, ROWS_FC, 128), lambda j: (0, j, 0, 0)),
            pl.BlockSpec((1, 16, 256, 128), lambda j: (j // 4, 0, 4 + j % 4, 0)),
            pl.BlockSpec((1, 512), lambda j: (0, j)),
            once((8, D), zero2),
        ],
        out_specs=[
            once((tok, D), zero2),
            once((tok, D), zero2),
            once((tok, D), zero2),
            once((32, ROWS_PROJ, 128), lambda j: (0, 0, 0)),
            pl.BlockSpec((2, 2, ROWS_FC, 128), lambda j: (0, j, 0, 0)),
            pl.BlockSpec((1, 16, 256, 128), lambda j: (j // 4, 0, j % 4, 0)),
            pl.BlockSpec((1, 512), lambda j: (0, j)),
            once((8, D), zero2),
        ],
        scratch_shapes=[
            pltpu.VMEM((tok, D), f32),
            pltpu.VMEM((tok, D), bf16),
            pltpu.VMEM((tok, D), bf16),
            pltpu.VMEM((tok, D), f32),
            pltpu.VMEM((D, 512), bf16),
            pltpu.VMEM((512, D), bf16),
            pltpu.VMEM((D, D), bf16),
        ],
        compiler_params=params(),
        cost_estimate=cost(2 * tok * D * (6 * FF + 3 * D), 60e6, tok * FF * 2),
        name="feed_forward_both",
    )(mixed, x_own, cot, gathered, by_block, by_block, bias1, vectors)


def project_back_body(tok, d0, d1, d2, x_own, x_oth, w00, w01, w10, w11, gain,
                      own_ref, oth_ref, gbias_ref, gvec_ref, w_sc, acc):
    step = pl.program_id(0)
    assemble_qkv(((w00, w01), (w10, w11)), w_sc)
    tile = jnp.concatenate([d0[...], d1[...], d2[...]], 1)
    gbias_ref[...] = jnp.sum(tile.astype(f32), axis=0, keepdims=True)

    @pl.when(step == 0)
    def _():
        acc[0:tok, :] = lax.dot_general(tile[0:tok], w_sc[...], NT, preferred_element_type=f32)
        acc[tok : 2 * tok, :] = jnp.zeros((tok, D), f32)

    @pl.when(step == 1)
    def _():
        acc[0:tok, :] += lax.dot_general(tile[0:tok], w_sc[...], NT, preferred_element_type=f32)

    @pl.when(step >= 2)
    def _():
        acc[...] += lax.dot_general(tile, w_sc[...], NT, preferred_element_type=f32)

    @pl.when(step == pl.num_programs(0) - 1)
    def _():
        first = jnp.zeros((1, D), f32)
        second = jnp.zeros((1, D), f32)
        for half, x_ref in enumerate((x_own, x_oth)):
            for i in range(tok // 112):
                rows = slice(i * 112, (i + 1) * 112)
                e = acc[half * tok + i * 112 : half * tok + (i + 1) * 112, :]
                normed, _ = row_stats(x_ref[rows, :].astype(f32))
                first = first + jnp.sum(e * normed, axis=0, keepdims=True)
                second = second + jnp.sum(e, axis=0, keepdims=True)
                if half == 0:
                    own_ref[rows, :] = e
                else:
                    oth_ref[rows, :] = e.astype(bf16)
        gvec_ref[...] = jnp.concatenate([first, second, jnp.zeros((6, D), f32)], 0)


def project_back_call(dqkv, x_own, x_oth, table, gathered, gain):
    tok = x_own.shape[0]

    def weight(r, k):
        return pl.BlockSpec((1, ROWS_A, 128), lambda j, t: (t[r * 16 + 2 * j + k], 0, 0))

    def piece(i):
        return pl.BlockSpec((None, 2 * tok, 128), lambda j, t: ((3 * j + i) // 8, 0, (3 * j + i) % 8))

    zero2 = lambda j, t: (0, 0)
    return pl.pallas_call(
        lambda t, *refs: project_back_body(tok, *refs),
        out_shape=(
            jax.ShapeDtypeStruct((tok, D), f32),
            jax.ShapeDtypeStruct((tok, D), bf16),
            jax.ShapeDtypeStruct((1, 3 * D), f32),
            jax.ShapeDtypeStruct((8, D), f32),
        ),
        grid_spec=pltpu.PrefetchScalarGridSpec(
            num_scalar_prefetch=1,
            grid=(8,),
            in_specs=[
                piece(0),
                piece(1),
                piece(2),
                once((tok, D), zero2),
                once((tok, D), zero2),
                weight(0, 0),
                weight(0, 1),
                weight(1, 0),
                weight(1, 1),
                once((1, D), zero2),
            ],
            out_specs=[
                once((tok, D), zero2),
                once((tok, D), zero2),
                pl.BlockSpec((1, 384), lambda j, t: (0, j)),
                once((8, D), zero2),
            ],
            scratch_shapes=[pltpu.VMEM((D, 384), bf16), pltpu.VMEM((2 * tok, D), f32)],
        ),
        compiler_params=params(),
        cost_estimate=cost(2 * tok * D * D * 5, 24e6),
        name="qkv_backward_tokens",
    )(table, dqkv, dqkv, dqkv, x_own, x_oth, gathered, gathered, gathered, gathered, gain)


def project_grad_body(tok, h_ref, d0, d1, d2, vec_ref, g_ref):
    step = pl.program_id(0)

    def write(rows):
        tile = jnp.concatenate([d0[0:rows], d1[0:rows], d2[0:rows]], 1)
        g = lax.dot_general(h_ref[0:rows, :], tile, TN, preferred_element_type=f32).astype(bf16)
        for r in range(2):
            lo, hi = g[512 * r : 512 * r + 256], g[512 * r + 256 : 512 * r + 512]
            g_ref[r, 0, 0:256] = lo[:, 0:128]
            g_ref[r, 0, 256:512] = hi[:, 0:128]
            g_ref[r, 0, 512:768] = jnp.concatenate([lo[:, 128:192], hi[:, 128:192]], 1)
            g_ref[r, 1, 0:256] = lo[:, 192:320]
            g_ref[r, 1, 256:512] = hi[:, 192:320]
            g_ref[r, 1, 512:768] = jnp.concatenate([lo[:, 320:384], hi[:, 320:384]], 1)

    @pl.when(step < 2)
    def _():
        write(tok)

    @pl.when(step >= 2)
    def _():
        write(2 * tok)

    g_ref[:, :, 768:784] = vec_ref[...]


def project_grad_call(hidden, dqkv, packed_vectors):
    both = hidden.shape[0]
    tok = both // 2

    def piece(i):
        return pl.BlockSpec((None, both, 128), lambda j: ((3 * j + i) // 8, 0, (3 * j + i) % 8))

    return pl.pallas_call(
        lambda *refs: project_grad_body(tok, *refs),
        out_shape=jax.ShapeDtypeStruct((2, 16, ROWS_A, 128), bf16),
        grid=(8,),
        in_specs=[
            once((both, D), lambda j: (0, 0)),
            piece(0),
            piece(1),
            piece(2),
            pl.BlockSpec((2, 2, 16, 128), lambda j: (0, j, 0, 0)),
        ],
        out_specs=pl.BlockSpec((2, 2, ROWS_A, 128), lambda j: (0, j, 0, 0)),
        compiler_params=params(),
        cost_estimate=cost(2 * tok * D * D * 5, 20e6),
        name="qkv_backward_weights",
    )(hidden, dqkv, dqkv, dqkv, packed_vectors)


def finish_body(own_ref, recv_ref, dmid_ref, x_ref, gain, out_ref):
    e = own_ref[...] + recv_ref[...].astype(f32)
    normed, inverse = row_stats(x_ref[...].astype(f32))
    scaled = e * gain[...]
    first = jnp.mean(scaled, axis=-1, keepdims=True)
    second = jnp.mean(scaled * normed, axis=-1, keepdims=True)
    out_ref[...] = dmid_ref[...] + inverse * (scaled - first - normed * second)


def finish_call(own, recv, dmid, x_own, gain):
    tok = own.shape[0]
    block = pl.BlockSpec((112, D), lambda i: (i, 0))
    return pl.pallas_call(
        finish_body,
        out_shape=jax.ShapeDtypeStruct((tok, D), f32),
        grid=(tok // 112,),
        in_specs=[block, block, block, block, pl.BlockSpec((1, D), lambda i: (0, 0))],
        out_specs=block,
        compiler_params=params(),
        cost_estimate=cost(tok * D * 20, 13e6),
        name="first_norm_backward",
    )(own, recv, dmid, x_own, gain)


AXES = ("row", "col")


def swap_rows(value):
    return lax.ppermute(value, "row", [(0, 1), (1, 0)])


def gather_blocks(rows):
    return lax.all_gather(rows, AXES, axis=0, tiled=False)


def scatter_blocks(blocks):
    flat = blocks.reshape((-1,) + blocks.shape[-2:])
    return lax.psum_scatter(flat, AXES, scatter_dimension=0, tiled=False)


def fast_device(
    tokens, w_qkv, w_proj, w_fc1, w_fc2, ln1_gain, ln1_bias, q_bias, v_bias,
    proj_bias, ln2_gain, ln2_bias, fc1_bias, fc2_bias, cotangent,
):
    small = (ln1_gain, ln1_bias, q_bias, v_bias, proj_bias, ln2_gain, ln2_bias, fc2_bias)
    vec_rows = jnp.concatenate(small + (fc1_bias,)).reshape(3, 128)
    shard_a = jnp.concatenate([pack_qkv(w_qkv), jnp.pad(vec_rows, ((0, 13), (0, 0)))], axis=0)
    shard_b = jnp.concatenate([pack_fc1(w_fc1), pack_fc2(w_fc2), pack_proj(w_proj)], axis=0)
    x_oth = swap_rows(tokens)
    full_a = gather_blocks(shard_a)
    full_b = gather_blocks(shard_b)
    table = jnp.arange(32, dtype=jnp.int32)
    vecs = full_a[:, ROWS_QKV : ROWS_QKV + 3].reshape(2, 16, 384).transpose(1, 0, 2).reshape(32, 384)
    vecs = vecs.astype(f32)
    flat = vecs[:, :256].reshape(32, 8, 32).transpose(1, 0, 2).reshape(8, D)
    bias1 = vecs[:, 256:].reshape(1, FF)
    gain1, shift1, bias_q, bias_v = (flat[i : i + 1] for i in range(4))
    qkv_bias = jnp.concatenate([bias_q, jnp.zeros_like(bias_q), bias_v], axis=1)
    second = jnp.concatenate([flat[4:8], jnp.zeros((4, D), f32)], axis=0)

    hidden, qkv = qkv_call(tokens, x_oth, table, full_a, gain1, shift1, qkv_bias)
    mixed, logsum = attend_call(qkv, tokens.shape[0])
    out, dmid, datt, grad_p, grad_1, grad_2, gb1, gvec2 = feed_call(
        mixed, tokens, cotangent, full_b, bias1, second
    )
    rs_2 = scatter_blocks(grad_2)
    rs_1 = scatter_blocks(grad_1)
    rs_p = scatter_blocks(grad_p)
    dqkv = attend_back_call(qkv, datt, mixed, logsum)
    own, oth, gbias, gvec1 = project_back_call(dqkv, tokens, x_oth, table, full_a, gain1)
    recv = swap_rows(oth)
    sums = jnp.concatenate(
        [gvec1[0:2], gbias[:, :D], gbias[:, 2 * D :], gvec2[2:3], gvec2[0:2], gvec2[3:4]], axis=0
    )
    lanes = sums.reshape(8, 16, 2, 32).transpose(2, 1, 0, 3).reshape(2, 16, 2, 128)
    ff_lanes = gb1.reshape(16, 2, 1, 128).transpose(1, 0, 2, 3)
    packed = jnp.concatenate([lanes, ff_lanes, jnp.zeros((2, 16, 13, 128), f32)], axis=2).astype(bf16)
    rs_a = scatter_blocks(project_grad_call(hidden, dqkv, packed))
    grad_inputs = finish_call(own, recv, dmid, tokens, gain1)
    vec = rs_a[ROWS_QKV : ROWS_QKV + 3].reshape(384).astype(f32)
    pieces = [vec[32 * i : 32 * i + 32] for i in range(8)]
    return (
        out,
        grad_inputs,
        unpack_qkv(rs_a).astype(f32),
        unpack_proj(rs_p).astype(f32),
        unpack_fc1(rs_1).astype(f32),
        unpack_fc2(rs_2).astype(f32),
        *pieces[:7],
        vec[256:384],
        pieces[7],
    )


def solution(mesh):
    fast = dict(mesh.shape) == {"row": 2, "col": 16}
    return jax.shard_map(
        fast_device if fast else per_device,
        mesh=mesh,
        in_specs=(
            P(("col", "row"), None),
            P("row", "col"),
            P("row", "col"),
            P("row", "col"),
            P("row", "col"),
            P(("col", "row")),
            P(("col", "row")),
            P(("col", "row")),
            P(("col", "row")),
            P(("col", "row")),
            P(("col", "row")),
            P(("col", "row")),
            P(("col", "row")),
            P(("col", "row")),
            P(("col", "row"), None),
        ),
        out_specs=(
            P(("col", "row"), None),
            P(("col", "row"), None),
            P("row", "col"),
            P("row", "col"),
            P("row", "col"),
            P("row", "col"),
            P(("col", "row")),
            P(("col", "row")),
            P(("col", "row")),
            P(("col", "row")),
            P(("col", "row")),
            P(("col", "row")),
            P(("col", "row")),
            P(("col", "row")),
            P(("col", "row")),
        ),
        check_vma=False,
    )
```

```python
import functools
import math

import jax
import jax.numpy as jnp
from jax import lax
from jax.experimental import pallas as pl
from jax.experimental.pallas import tpu as pltpu
from jax.sharding import PartitionSpec as P

D = 1024
H = 16
HD = 64
LEN = 1568


EPSILON = 1e-06


def layer_norm(value, gain, shift):
    average = jnp.mean(value, axis=-1, keepdims=True)
    centred = value - average
    spread = jnp.mean(centred * centred, axis=-1, keepdims=True)
    inverse = lax.rsqrt(spread + EPSILON)
    normed = centred * inverse
    return (normed * gain + shift, normed, inverse)


def norm_back(grad_out, normed, inverse, gain):
    scaled = grad_out * gain
    mean_first = jnp.mean(scaled, axis=-1, keepdims=True)
    mean_second = jnp.mean(scaled * normed, axis=-1, keepdims=True)
    return inverse * (scaled - mean_first - normed * mean_second)


def gelu_slope(pre_act):
    cumulative = 0.5 * (1.0 + lax.erf(pre_act * 2.0 ** (-0.5)))
    density = jnp.exp(-0.5 * pre_act * pre_act) * (2.0 * math.pi) ** (-0.5)
    return cumulative + pre_act * density


def inner_rows(first, second):
    return lax.dot_general(
        first, second, (((0,), (0,)), ((), ())), preferred_element_type=jnp.float32
    )


def outer_cols(first, second):
    return lax.dot_general(
        first, second, (((1,), (1,)), ((), ())), preferred_element_type=jnp.float32
    )


def clip_forward(block):
    queries, key_rows, value_rows = (block[:, 0], block[:, 1], block[:, 2])
    scores = jnp.einsum(
        "qhd,khd->hqk", queries, key_rows, preferred_element_type=jnp.float32
    ) * HD ** (-0.5)
    row_peak = jnp.max(scores, axis=-1, keepdims=True)
    exponent = jnp.exp(scores - row_peak)
    row_total = jnp.sum(exponent, axis=-1, keepdims=True)
    weights_low = (exponent / row_total).astype(jnp.bfloat16)
    mixed_heads = jnp.einsum(
        "hqk,khd->qhd", weights_low, value_rows, preferred_element_type=jnp.float32
    )
    return (mixed_heads.astype(jnp.bfloat16), (row_peak + jnp.log(row_total))[..., 0])


def clip_backward(element):
    block, grad_mixed, logsum = element
    queries, key_rows, value_rows = (block[:, 0], block[:, 1], block[:, 2])
    scores = jnp.einsum(
        "qhd,khd->hqk", queries, key_rows, preferred_element_type=jnp.float32
    ) * HD ** (-0.5)
    weights_full = jnp.exp(scores - logsum[..., None])
    weights_low = weights_full.astype(jnp.bfloat16)
    grad_values = jnp.einsum(
        "hqk,qhd->khd", weights_low, grad_mixed, preferred_element_type=jnp.float32
    )
    grad_weights = jnp.einsum(
        "qhd,khd->hqk", grad_mixed, value_rows, preferred_element_type=jnp.float32
    )
    row_delta = jnp.sum(grad_weights * weights_full, axis=-1, keepdims=True)
    grad_scores = (weights_full * (grad_weights - row_delta)).astype(jnp.bfloat16)
    grad_queries = jnp.einsum(
        "hqk,khd->qhd", grad_scores, key_rows, preferred_element_type=jnp.float32
    ) * HD ** (-0.5)
    grad_keys = jnp.einsum(
        "hqk,qhd->khd", grad_scores, queries, preferred_element_type=jnp.float32
    ) * HD ** (-0.5)
    return jnp.stack([grad_queries, grad_keys, grad_values], axis=1).astype(jnp.bfloat16)


def per_device(
    tokens,
    w_qkv,
    w_proj,
    w_fc1,
    w_fc2,
    ln1_gain,
    ln1_bias,
    q_bias,
    v_bias,
    proj_bias,
    ln2_gain,
    ln2_bias,
    fc1_bias,
    fc2_bias,
    cotangent,
):
    (
        qkv_part,
        proj_part,
        fc1_part,
        fc2_part,
        gain1_part,
        shift1_part,
        biasq_part,
        biasv_part,
        biasp_part,
        gain2_part,
        shift2_part,
        bias1_part,
        bias2_part,
    ) = (
        lax.all_gather(w_qkv, "row", axis=0, tiled=True),
        lax.all_gather(w_proj, "row", axis=0, tiled=True),
        lax.all_gather(w_fc1, "row", axis=0, tiled=True),
        lax.all_gather(w_fc2, "row", axis=0, tiled=True),
        lax.all_gather(ln1_gain, "row", axis=0, tiled=True),
        lax.all_gather(ln1_bias, "row", axis=0, tiled=True),
        lax.all_gather(q_bias, "row", axis=0, tiled=True),
        lax.all_gather(v_bias, "row", axis=0, tiled=True),
        lax.all_gather(proj_bias, "row", axis=0, tiled=True),
        lax.all_gather(ln2_gain, "row", axis=0, tiled=True),
        lax.all_gather(ln2_bias, "row", axis=0, tiled=True),
        lax.all_gather(fc1_bias, "row", axis=0, tiled=True),
        lax.all_gather(fc2_bias, "row", axis=0, tiled=True),
    )
    (
        full_qkv,
        full_proj,
        full_fc1,
        full_fc2,
        full_gain1,
        full_shift1,
        full_biasq,
        full_biasv,
        full_biasp,
        full_gain2,
        full_shift2,
        full_bias1,
        full_bias2,
    ) = (
        lax.all_gather(qkv_part, "col", axis=1, tiled=True),
        lax.all_gather(proj_part, "col", axis=1, tiled=True),
        lax.all_gather(fc1_part, "col", axis=1, tiled=True),
        lax.all_gather(fc2_part, "col", axis=1, tiled=True),
        lax.all_gather(gain1_part, "col", axis=0, tiled=True),
        lax.all_gather(shift1_part, "col", axis=0, tiled=True),
        lax.all_gather(biasq_part, "col", axis=0, tiled=True),
        lax.all_gather(biasv_part, "col", axis=0, tiled=True),
        lax.all_gather(biasp_part, "col", axis=0, tiled=True),
        lax.all_gather(gain2_part, "col", axis=0, tiled=True),
        lax.all_gather(shift2_part, "col", axis=0, tiled=True),
        lax.all_gather(bias1_part, "col", axis=0, tiled=True),
        lax.all_gather(bias2_part, "col", axis=0, tiled=True),
    )
    gain_first = full_gain1.astype(jnp.float32)
    gain_second = full_gain2.astype(jnp.float32)
    groups = lax.axis_size("row")
    heads_local = H // groups
    per_group = heads_local * HD
    inputs = tokens.astype(jnp.float32)
    token_rows = inputs.shape[0]
    normed_out1, normed_one, inverse_one = layer_norm(
        inputs, gain_first, full_shift1.astype(jnp.float32)
    )
    hidden_one = normed_out1.astype(jnp.bfloat16)
    bias_q = full_biasq.astype(jnp.float32)
    qkv_bias = jnp.concatenate([bias_q, jnp.zeros_like(bias_q), full_biasv.astype(jnp.float32)])
    projected = jnp.dot(hidden_one, full_qkv, preferred_element_type=jnp.float32) + qkv_bias
    qkv_low = projected.astype(jnp.bfloat16).reshape(token_rows, 3, groups, per_group)
    by_heads = lax.all_to_all(qkv_low, "row", split_axis=2, concat_axis=0, tiled=True)
    col_rows = by_heads.shape[0]
    clip_count = col_rows // LEN
    blocks = by_heads.reshape(clip_count, LEN, 3, heads_local, HD)
    mixed_heads, logsum = lax.map(clip_forward, blocks)
    attended = lax.all_to_all(
        mixed_heads.reshape(col_rows, 1, per_group), "row", split_axis=0, concat_axis=1, tiled=True
    ).reshape(token_rows, D)
    middle = inputs + (
        jnp.dot(attended, full_proj, preferred_element_type=jnp.float32)
        + full_biasp.astype(jnp.float32)
    )
    normed_out2, normed_two, inverse_two = layer_norm(
        middle, gain_second, full_shift2.astype(jnp.float32)
    )
    hidden_two = normed_out2.astype(jnp.bfloat16)
    pre_act = jnp.dot(hidden_two, full_fc1, preferred_element_type=jnp.float32) + full_bias1.astype(
        jnp.float32
    )
    activated = jax.nn.gelu(pre_act, approximate=False).astype(jnp.bfloat16)
    result = middle + (
        jnp.dot(activated, full_fc2, preferred_element_type=jnp.float32)
        + full_bias2.astype(jnp.float32)
    )
    qkv_again, proj_again, fc1_again, fc2_again = (
        lax.all_gather(w_qkv, "row", axis=0, tiled=True),
        lax.all_gather(w_proj, "row", axis=0, tiled=True),
        lax.all_gather(w_fc1, "row", axis=0, tiled=True),
        lax.all_gather(w_fc2, "row", axis=0, tiled=True),
    )
    back_qkv, back_proj, back_fc1, back_fc2 = (
        lax.all_gather(qkv_again, "col", axis=1, tiled=True),
        lax.all_gather(proj_again, "col", axis=1, tiled=True),
        lax.all_gather(fc1_again, "col", axis=1, tiled=True),
        lax.all_gather(fc2_again, "col", axis=1, tiled=True),
    )
    grad_out = cotangent.astype(jnp.bfloat16)
    grad_bias2 = jnp.sum(grad_out.astype(jnp.float32), axis=0)
    grad_fc2 = inner_rows(activated, grad_out)
    grad_act = outer_cols(grad_out, back_fc2)
    grad_pre = (grad_act * gelu_slope(pre_act)).astype(jnp.bfloat16)
    grad_bias1 = jnp.sum(grad_pre.astype(jnp.float32), axis=0)
    grad_fc1 = inner_rows(hidden_two, grad_pre)
    grad_hidden2 = outer_cols(grad_pre, back_fc1)
    grad_gain2 = jnp.sum(grad_hidden2 * normed_two, axis=0)
    grad_shift2 = jnp.sum(grad_hidden2, axis=0)
    grad_middle = cotangent + norm_back(grad_hidden2, normed_two, inverse_two, gain_second)
    grad_branch = grad_middle.astype(jnp.bfloat16)
    grad_biasp = jnp.sum(grad_branch.astype(jnp.float32), axis=0)
    grad_proj = inner_rows(attended, grad_branch)
    grad_attended = outer_cols(grad_branch, back_proj).astype(jnp.bfloat16)
    grad_heads = lax.all_to_all(
        grad_attended.reshape(token_rows, groups, per_group),
        "row",
        split_axis=1,
        concat_axis=0,
        tiled=True,
    )
    grad_blocks = grad_heads.reshape(clip_count, LEN, heads_local, HD)
    grad_triple = lax.map(clip_backward, (blocks, grad_blocks, logsum))
    grad_tokens_qkv = lax.all_to_all(
        grad_triple.reshape(col_rows, 3, 1, per_group),
        "row",
        split_axis=0,
        concat_axis=2,
        tiled=True,
    ).reshape(token_rows, 3 * D)
    grad_qkv_float = grad_tokens_qkv.astype(jnp.float32)
    grad_biasq = jnp.sum(grad_qkv_float[:, :D], axis=0)
    grad_biasv = jnp.sum(grad_qkv_float[:, 2 * D :], axis=0)
    grad_qkv = inner_rows(hidden_one, grad_tokens_qkv)
    grad_hidden1 = outer_cols(grad_tokens_qkv, back_qkv)
    grad_gain1 = jnp.sum(grad_hidden1 * normed_one, axis=0)
    grad_shift1 = jnp.sum(grad_hidden1, axis=0)
    grad_inputs = grad_middle + norm_back(grad_hidden1, normed_one, inverse_one, gain_first)
    (
        sum_qkv,
        sum_proj,
        sum_fc1,
        sum_fc2,
        sum_gain1,
        sum_shift1,
        sum_biasq,
        sum_biasv,
        sum_biasp,
        sum_gain2,
        sum_shift2,
        sum_bias1,
        sum_bias2,
    ) = (
        lax.psum_scatter(
            grad_qkv.astype(jnp.bfloat16), "col", scatter_dimension=1, tiled=True
        ).astype(jnp.float32),
        lax.psum_scatter(
            grad_proj.astype(jnp.bfloat16), "col", scatter_dimension=1, tiled=True
        ).astype(jnp.float32),
        lax.psum_scatter(
            grad_fc1.astype(jnp.bfloat16), "col", scatter_dimension=1, tiled=True
        ).astype(jnp.float32),
        lax.psum_scatter(
            grad_fc2.astype(jnp.bfloat16), "col", scatter_dimension=1, tiled=True
        ).astype(jnp.float32),
        lax.psum_scatter(
            grad_gain1.astype(jnp.bfloat16), "col", scatter_dimension=0, tiled=True
        ).astype(jnp.float32),
        lax.psum_scatter(
            grad_shift1.astype(jnp.bfloat16), "col", scatter_dimension=0, tiled=True
        ).astype(jnp.float32),
        lax.psum_scatter(
            grad_biasq.astype(jnp.bfloat16), "col", scatter_dimension=0, tiled=True
        ).astype(jnp.float32),
        lax.psum_scatter(
            grad_biasv.astype(jnp.bfloat16), "col", scatter_dimension=0, tiled=True
        ).astype(jnp.float32),
        lax.psum_scatter(
            grad_biasp.astype(jnp.bfloat16), "col", scatter_dimension=0, tiled=True
        ).astype(jnp.float32),
        lax.psum_scatter(
            grad_gain2.astype(jnp.bfloat16), "col", scatter_dimension=0, tiled=True
        ).astype(jnp.float32),
        lax.psum_scatter(
            grad_shift2.astype(jnp.bfloat16), "col", scatter_dimension=0, tiled=True
        ).astype(jnp.float32),
        lax.psum_scatter(
            grad_bias1.astype(jnp.bfloat16), "col", scatter_dimension=0, tiled=True
        ).astype(jnp.float32),
        lax.psum_scatter(
            grad_bias2.astype(jnp.bfloat16), "col", scatter_dimension=0, tiled=True
        ).astype(jnp.float32),
    )
    (
        out_qkv,
        out_proj,
        out_fc1,
        out_fc2,
        out_gain1,
        out_shift1,
        out_biasq,
        out_biasv,
        out_biasp,
        out_gain2,
        out_shift2,
        out_bias1,
        out_bias2,
    ) = (
        lax.psum_scatter(
            sum_qkv.astype(jnp.bfloat16), "row", scatter_dimension=0, tiled=True
        ).astype(jnp.float32),
        lax.psum_scatter(
            sum_proj.astype(jnp.bfloat16), "row", scatter_dimension=0, tiled=True
        ).astype(jnp.float32),
        lax.psum_scatter(
            sum_fc1.astype(jnp.bfloat16), "row", scatter_dimension=0, tiled=True
        ).astype(jnp.float32),
        lax.psum_scatter(
            sum_fc2.astype(jnp.bfloat16), "row", scatter_dimension=0, tiled=True
        ).astype(jnp.float32),
        lax.psum_scatter(
            sum_gain1.astype(jnp.bfloat16), "row", scatter_dimension=0, tiled=True
        ).astype(jnp.float32),
        lax.psum_scatter(
            sum_shift1.astype(jnp.bfloat16), "row", scatter_dimension=0, tiled=True
        ).astype(jnp.float32),
        lax.psum_scatter(
            sum_biasq.astype(jnp.bfloat16), "row", scatter_dimension=0, tiled=True
        ).astype(jnp.float32),
        lax.psum_scatter(
            sum_biasv.astype(jnp.bfloat16), "row", scatter_dimension=0, tiled=True
        ).astype(jnp.float32),
        lax.psum_scatter(
            sum_biasp.astype(jnp.bfloat16), "row", scatter_dimension=0, tiled=True
        ).astype(jnp.float32),
        lax.psum_scatter(
            sum_gain2.astype(jnp.bfloat16), "row", scatter_dimension=0, tiled=True
        ).astype(jnp.float32),
        lax.psum_scatter(
            sum_shift2.astype(jnp.bfloat16), "row", scatter_dimension=0, tiled=True
        ).astype(jnp.float32),
        lax.psum_scatter(
            sum_bias1.astype(jnp.bfloat16), "row", scatter_dimension=0, tiled=True
        ).astype(jnp.float32),
        lax.psum_scatter(
            sum_bias2.astype(jnp.bfloat16), "row", scatter_dimension=0, tiled=True
        ).astype(jnp.float32),
    )
    return (
        result.astype(jnp.bfloat16),
        grad_inputs,
        out_qkv,
        out_proj,
        out_fc1,
        out_fc2,
        out_gain1,
        out_shift1,
        out_biasq,
        out_biasv,
        out_biasp,
        out_gain2,
        out_shift2,
        out_bias1,
        out_bias2,
    )


bf16 = jnp.bfloat16
f32 = jnp.float32
FF = 4096
ROWS_QKV, ROWS_A = 768, 784
ROWS_FC, ROWS_PROJ, ROWS_B = 1024, 256, 2304
VMEM_LIMIT = 62 * 1024 * 1024
NT = (((1,), (1,)), ((), ()))
TN = (((0,), (0,)), ((), ()))


def params(limit=VMEM_LIMIT):
    return pltpu.CompilerParams(vmem_limit_bytes=limit)


def cost(flops, data, trans=0):
    return pl.CostEstimate(flops=int(flops), bytes_accessed=int(data), transcendentals=int(trans))


def once(shape, index):
    return pl.BlockSpec(shape, index, pipeline_mode=pl.Buffered(1))


def halves_cat(first, second):
    return jnp.concatenate([first[:, :64], second[:, :64]], axis=1)


def row_stats(value):
    average = jnp.mean(value, axis=-1, keepdims=True)
    centred = value - average
    spread = jnp.mean(centred * centred, axis=-1, keepdims=True)
    inverse = lax.rsqrt(spread + EPSILON)
    return centred * inverse, inverse


def pack_a_body(w_ref, vec_ref, out_ref):
    w = w_ref[...]
    out_ref[0:512] = w[:, :128]
    out_ref[512:768] = jnp.concatenate([w[:256, 128:], w[256:, 128:]], 1)
    out_ref[768:784] = vec_ref[...]


def pack_a(w_qkv, vec_rows):
    return pl.pallas_call(
        pack_a_body,
        out_shape=jax.ShapeDtypeStruct((ROWS_A, 128), bf16),
        compiler_params=params(),
        cost_estimate=cost(1e5, 5e5),
        name="pack_first",
    )(w_qkv, vec_rows)


def pack_b_body(w1_ref, w2_ref, wp_ref, out_ref):
    w1 = w1_ref[...]
    out_ref[0:512] = w1[:, :128]
    out_ref[512:1024] = w1[:, 128:]
    for q in range(4):
        top, low = w2_ref[512 * q : 512 * q + 256], w2_ref[512 * q + 256 : 512 * q + 512]
        out_ref[1024 + 256 * q : 1280 + 256 * q] = jnp.concatenate([top, low], 1)
    out_ref[2048:2304] = jnp.concatenate([wp_ref[0:256], wp_ref[256:512]], 1)


def pack_b(w_fc1, w_fc2, w_proj):
    return pl.pallas_call(
        pack_b_body,
        out_shape=jax.ShapeDtypeStruct((ROWS_B, 128), bf16),
        compiler_params=params(),
        cost_estimate=cost(1e5, 1.5e6),
        name="pack_second",
    )(w_fc1, w_fc2, w_proj)


def total_of(refs):
    total = refs[0][0].astype(f32)
    for ref in refs[1:4]:
        total = total + ref[0].astype(f32)
    for ref in refs[4:]:
        total = total + ref[...].astype(f32)
    return total


def finish_a_body(*refs):
    total, outs = total_of(refs[:7]), refs[7:]
    outs[0][:, 0:128] = total[0:512]
    outs[0][0:256, 128:192] = total[512:768, :64]
    outs[0][256:512, 128:192] = total[512:768, 64:]
    for i in range(8):
        row, lane = i // 4, 32 * (i % 4)
        outs[1 + i][...] = total[768 + row : 769 + row, lane : lane + 32]
    outs[9][...] = total[770:771]


def finish_1_body(*refs):
    total = total_of(refs[:7])
    refs[7][:, 0:128] = total[0:512]
    refs[7][:, 128:256] = total[512:1024]


def finish_2_body(*refs):
    total = total_of(refs[:7])
    for q in range(4):
        piece = total[256 * q : 256 * q + 256]
        refs[7][512 * q : 512 * q + 256] = piece[:, :64]
        refs[7][512 * q + 256 : 512 * q + 512] = piece[:, 64:]


def finish_p_body(ref, out_ref):
    piece = ref[...].astype(f32)
    out_ref[0:256] = piece[:, :64]
    out_ref[256:512] = piece[:, 64:]


def finish_sum(body, terms, shapes, name):
    rows = terms[-1].shape[0]
    block = pl.BlockSpec((1, rows, 128), lambda i: (0, 0, 0))
    single = pl.BlockSpec((rows, 128), lambda i: (0, 0))
    return pl.pallas_call(
        body,
        out_shape=tuple(jax.ShapeDtypeStruct(shape, f32) for shape in shapes),
        grid=(1,),
        in_specs=[block] * 4 + [single] * 3,
        out_specs=tuple(pl.BlockSpec(shape, lambda i: (0, 0)) for shape in shapes),
        compiler_params=params(),
        cost_estimate=cost(1e6, 3e6),
        name=name,
    )(*terms)


def assemble_qkv(core, w_refs, w_out):
    for r in range(2):
        mine, theirs = w_refs[r][0][0], w_refs[r][1][0]
        w0 = jnp.where(core == 0, mine, theirs)
        w1 = jnp.where(core == 0, theirs, mine)
        a0, b0 = w0[:512], w0[512:768]
        a1, b1 = w1[:512], w1[512:768]
        lo = slice(512 * r, 512 * r + 256)
        hi = slice(512 * r + 256, 512 * r + 512)
        w_out[512 * r : 512 * r + 512, 0:128] = a0
        w_out[lo, 128:256] = jnp.concatenate([b0[:, :64], a1[:256, :64]], axis=1)
        w_out[hi, 128:256] = jnp.concatenate([b0[:, 64:], a1[256:, :64]], axis=1)
        w_out[lo, 256:384] = jnp.concatenate([a1[:256, 64:], b1[:, :64]], axis=1)
        w_out[hi, 256:384] = jnp.concatenate([a1[256:, 64:], b1[:, 64:]], axis=1)


def qkv_body(tok, tab, x_own, x_oth, w00, w01, w10, w11, gain, shift, bias, h_ref, qkv_ref, w_sc):
    step = pl.program_id(0)

    @pl.when(step == 0)
    def _():
        for half, x_ref in enumerate((x_own, x_oth)):
            for i in range(tok // 112):
                rows = x_ref[i * 112 : (i + 1) * 112, :].astype(f32)
                normed, _ = row_stats(rows)
                h_ref[half * tok + i * 112 : half * tok + (i + 1) * 112, :] = (
                    normed * gain[...] + shift[...]
                ).astype(bf16)

    assemble_qkv(tab[32], ((w00, w01), (w10, w11)), w_sc)

    def project(rows):
        out = jnp.dot(h_ref[0:rows, :], w_sc[...], preferred_element_type=f32) + bias[...]
        out = out.astype(bf16)
        for i in range(3):
            tile = 3 * step + i
            part, column = tile // 8, tile % 8
            qkv_ref[part, 0:rows, pl.ds(pl.multiple_of(column * 128, 128), 128)] = out[
                :, i * 128 : (i + 1) * 128
            ]

    @pl.when(step < 2)
    def _():
        project(tok)

    @pl.when(step >= 2)
    def _():
        project(2 * tok)


def qkv_call(x_own, x_oth, table, mine, theirs, gain, shift, bias):
    tok = x_own.shape[0]

    def weight(r, k):
        return pl.BlockSpec((1, ROWS_A, 128), lambda j, t: (t[k * 16 + r * 8 + j], 0, 0))

    return pl.pallas_call(
        functools.partial(qkv_body, tok),
        out_shape=(
            jax.ShapeDtypeStruct((2 * tok, D), bf16),
            jax.ShapeDtypeStruct((3, 2 * tok, D), bf16),
        ),
        grid_spec=pltpu.PrefetchScalarGridSpec(
            num_scalar_prefetch=1,
            grid=(8,),
            in_specs=[
                once((tok, D), lambda j, t: (0, 0)),
                once((tok, D), lambda j, t: (0, 0)),
                weight(0, 0),
                weight(0, 1),
                weight(1, 0),
                weight(1, 1),
                once((1, D), lambda j, t: (0, 0)),
                once((1, D), lambda j, t: (0, 0)),
                pl.BlockSpec((1, 384), lambda j, t: (0, j)),
            ],
            out_specs=[
                once((2 * tok, D), lambda j, t: (0, 0)),
                once((3, 2 * tok, D), lambda j, t: (0, 0, 0)),
            ],
            scratch_shapes=[pltpu.VMEM((D, 384), bf16)],
        ),
        compiler_params=params(),
        cost_estimate=cost(2 * tok * D * D * 5, 24e6),
        name="qkv_forward",
    )(table, x_own, x_oth, mine, theirs, mine, theirs, gain, shift, bias)


def attend_body(tok, keys, chunk, q_ref, k_ref, v_ref, o_ref, l_ref, *scratch):
    vt_a, vt_b, qm, s_a, s_b, m_a, m_b, acc_sc, o_sc = scratch
    count = keys // chunk
    lane = lax.broadcasted_iota(jnp.int32, (1, 128), 1)
    q2 = q_ref[...] * jnp.asarray(HD**-0.5, bf16)
    zero = jnp.zeros_like(q2)

    def stage(q_head, s_w, m_w, s_r, m_r, vt_r):
        peak = jnp.max(m_r[...], axis=0, keepdims=True)
        acc_sc[...] = jnp.zeros_like(acc_sc)
        qm[...] = q_head
        m_w[...] = jnp.full_like(m_w, -jnp.inf)
        for i in range(count):
            rows = slice(i * chunk, (i + 1) * chunk)
            s = lax.dot_general(k_ref[rows, :], qm[...], NT, preferred_element_type=f32)
            s_w[rows, :] = s
            m_w[...] = jnp.maximum(m_w[...], jnp.max(s.reshape(chunk // 8, 8, tok), axis=0))
            p = jnp.exp(s_r[rows, :] - peak).astype(bf16)
            acc_sc[...] += jnp.dot(vt_r[i], p, preferred_element_type=f32)
        acc = acc_sc[...]
        total = acc[64:65]
        return acc[0:64] * (1.0 / total), peak + jnp.log(total)

    out_b, lse_b = stage(jnp.where(lane < 64, q2, zero), s_a, m_a, s_b, m_b, vt_b)
    o_ref[0:64] = o_sc[0:64].astype(bf16)
    o_ref[64:128] = out_b.astype(bf16)
    l_ref[0] = o_sc[64:65]
    l_ref[1] = lse_b
    ones = jnp.ones((16, chunk), bf16)
    for i in range(count):
        vt = v_ref[i * chunk : (i + 1) * chunk, :].T
        vt_a[i, 0:64] = vt[0:64]
        vt_a[i, 64:80] = ones
        vt_b[i, 0:64] = vt[64:128]
        vt_b[i, 64:80] = ones
    out_a, lse_a = stage(jnp.where(lane < 64, zero, q2), s_b, m_b, s_a, m_a, vt_a)
    o_sc[0:64] = out_a
    o_sc[64:65] = lse_a


def attend_call(qkv, tok, chunk=224):
    keys = qkv.shape[1]
    pairs = H // 2

    def column(part, rows):
        return pl.BlockSpec((None, rows, 128), lambda g: (part, 0, jnp.minimum(g, pairs - 1)))

    def behind(g):
        return jnp.maximum(g - 1, 0)

    return pl.pallas_call(
        lambda *refs: attend_body(tok, keys, chunk, *refs),
        out_shape=(
            jax.ShapeDtypeStruct((D, tok), bf16),
            jax.ShapeDtypeStruct((H, 1, tok), f32),
        ),
        grid=(pairs + 1,),
        in_specs=[column(0, tok), column(1, keys), column(2, keys)],
        out_specs=[
            pl.BlockSpec((128, tok), lambda g: (behind(g), 0)),
            pl.BlockSpec((2, 1, tok), lambda g: (behind(g), 0, 0)),
        ],
        scratch_shapes=[
            pltpu.VMEM((keys // chunk, 80, chunk), bf16),
            pltpu.VMEM((keys // chunk, 80, chunk), bf16),
            pltpu.VMEM((tok, 128), bf16),
            pltpu.VMEM((keys, tok), f32),
            pltpu.VMEM((keys, tok), f32),
            pltpu.VMEM((8, tok), f32),
            pltpu.VMEM((8, tok), f32),
            pltpu.VMEM((80, tok), f32),
            pltpu.VMEM((72, tok), f32),
        ],
        compiler_params=params(),
        cost_estimate=cost(16 * 4 * tok * keys * 256, 12e6, 16 * tok * keys),
        name="attention_forward",
    )(qkv, qkv, qkv)


def attend_back_body(tok, keys, chunk, q_ref, k_ref, v_ref, g_ref, o_ref, l_ref, *rest):
    out_ref, *scratch = rest[-6:]
    qx, gx, q_t, g_t, dq_sc = scratch
    lane = lax.broadcasted_iota(jnp.int32, (1, 128), 1)
    row = lax.broadcasted_iota(jnp.int32, (128, 1), 0)
    q2 = q_ref[...] * jnp.asarray(HD**-0.5, bf16)
    grad = g_ref[...]
    qx[:, 0:128] = q2
    gx[:, 0:128] = grad
    q_t[...] = q2.T
    g_t[...] = grad.T
    prod = g_t[...].astype(f32) * o_ref[...].astype(f32)

    def split(value):
        terms, rest = [], value
        for _ in range(3):
            term = rest.astype(bf16).astype(f32)
            terms.append(term)
            rest = rest - term
        return terms

    s_col = jnp.zeros((128, tok), f32)
    d_col = jnp.zeros((128, tok), f32)
    for h in range(2):
        delta = jnp.sum(prod[h * 64 : h * 64 + 64], axis=0, keepdims=True)
        for t, (a, b) in enumerate(zip(split(-l_ref[h]), split(-delta))):
            s_col = jnp.where(row == h * 4 + t, a, s_col)
            d_col = jnp.where(row == h * 4 + t, b, d_col)
    qx[:, 128:256] = s_col.astype(bf16).T
    gx[:, 128:256] = d_col.astype(bf16).T
    dq_sc[...] = jnp.zeros_like(dq_sc)
    for i in range(keys // chunk):
        rows = slice(i * chunk, (i + 1) * chunk)
        ks, vs = k_ref[rows, :], v_ref[rows, :]
        dvs, dks, dq = [], [], None
        for h in range(2):
            mine = (lane >= h * 64) & (lane < h * 64 + 64)
            pick = jnp.broadcast_to(
                ((lane >= h * 4) & (lane < h * 4 + 3)).astype(bf16), (chunk, 128)
            )
            km = jnp.where(mine, ks, jnp.zeros_like(ks))
            vm = jnp.where(mine, vs, jnp.zeros_like(vs))
            p = jnp.exp(
                lax.dot_general(
                    qx[...], jnp.concatenate([km, pick], 1), NT, preferred_element_type=f32
                )
            )
            dp = lax.dot_general(
                gx[...], jnp.concatenate([vm, pick], 1), NT, preferred_element_type=f32
            )
            ds = (p * dp).astype(bf16)
            p_low = p.astype(bf16)
            head = slice(h * 64, h * 64 + 64)
            dvs.append(jnp.dot(g_t[head], p_low, preferred_element_type=f32))
            dks.append(jnp.dot(q_t[head], ds, preferred_element_type=f32))
            part = jnp.dot(ds, km, preferred_element_type=f32)
            dq = part if dq is None else dq + part
        dq_sc[...] += dq
        out_ref[1, rows, :] = jnp.concatenate(dks, 0).T.astype(bf16)
        out_ref[2, rows, :] = jnp.concatenate(dvs, 0).T.astype(bf16)
    out_ref[0, 0:tok, :] = (dq_sc[...] * HD**-0.5).astype(bf16)
    out_ref[0, tok:keys, :] = jnp.zeros((keys - tok, 128), bf16)


def attend_back_call(qkv, grad, mixed, logsum, pieces=4, chunk=224):
    tok = grad.shape[0]
    keys = qkv.shape[1]
    count = H // 2 // pieces
    out = None
    for first in range(0, H // 2, count):

        def column(part, rows, first=first):
            return pl.BlockSpec((None, rows, 128), lambda g: (part, 0, first + g))

        out = pl.pallas_call(
            functools.partial(attend_back_body, tok, keys, chunk),
            out_shape=jax.ShapeDtypeStruct((3, keys, D), bf16),
            grid=(count,),
            in_specs=[
                column(0, tok),
                column(1, keys),
                column(2, keys),
                pl.BlockSpec((tok, 128), lambda g, first=first: (0, first + g)),
                pl.BlockSpec((128, tok), lambda g, first=first: (first + g, 0)),
                pl.BlockSpec((2, 1, tok), lambda g, first=first: (first + g, 0, 0)),
            ]
            + ([] if out is None else [pl.BlockSpec(memory_space=pl.ANY)]),
            out_specs=pl.BlockSpec((3, keys, 128), lambda g, first=first: (0, 0, first + g)),
            scratch_shapes=[
                pltpu.VMEM((tok, 256), bf16),
                pltpu.VMEM((tok, 256), bf16),
                pltpu.VMEM((128, tok), bf16),
                pltpu.VMEM((128, tok), bf16),
                pltpu.VMEM((tok, 128), f32),
            ],
            input_output_aliases={} if out is None else {6: 0},
            compiler_params=params(),
            cost_estimate=cost(
                16 * 8 * tok * keys * 256 / pieces, 24e6 / pieces, 16 * tok * keys / pieces
            ),
            name="attention_backward",
        )(qkv, qkv, qkv, grad, mixed, logsum, *(() if out is None else (out,)))
    return out


def gelu_parts(value):
    size = jnp.abs(value)
    bell = jnp.exp(-0.5 * value * value)
    t = 1.0 / (1.0 + (0.3275911 * 2.0**-0.5) * size)
    poly = t * (
        0.254829592
        + t * (-0.284496736 + t * (1.421413741 + t * (-1.453152027 + t * 1.061405429)))
    )
    upper = 0.5 * poly * bell
    phi = jnp.where(value >= 0.0, 1.0 - upper, upper)
    return value * phi, phi + value * (bell * (2.0 * math.pi) ** -0.5)


def feed_body(
    tok, tab, o_ref, x_ref, cot_ref, wp_ref, w1_ref, w2_ref, b1_ref, vec_ref,
    out_ref, dmid_ref, datt_ref, gp_ref, m1_ref, t1_ref, m2_ref, t2_ref, gb1_ref, gvec_ref,
    mid, h2, dm, y_acc, w1, w2, wp, dpre_sc, g2_sc,
):
    step, inner = pl.program_id(0), pl.program_id(1)
    last = pl.num_programs(0) - 1
    part = 112
    pieces = [slice(i * part, (i + 1) * part) for i in range(tok // part)]

    @pl.when((step == 0) & (inner == 0))
    def _():
        for r in range(2):
            for c in range(8):
                p0, p1 = wp_ref[r * 16 + 2 * c], wp_ref[r * 16 + 2 * c + 1]
                cols = slice(128 * c, 128 * c + 128)
                wp[512 * r : 512 * r + 256, cols] = jnp.concatenate([p0[:, :64], p1[:, :64]], 1)
                wp[512 * r + 256 : 512 * r + 512, cols] = jnp.concatenate([p0[:, 64:], p1[:, 64:]], 1)
        mid[...] = lax.dot_general(o_ref[...], wp[...], TN, preferred_element_type=f32)
        for rows in pieces:
            total = x_ref[rows, :].astype(f32) + (mid[rows, :] + vec_ref[0:1, :])
            mid[rows, :] = total
            normed, _ = row_stats(total)
            h2[rows, :] = (normed * vec_ref[1:2, :] + vec_ref[2:3, :]).astype(bf16)
            dm[rows, :] = cot_ref[rows, :].astype(bf16)

    @pl.when(inner == 0)
    def _():
        for r in range(2):
            for k in range(2):
                for s in range(2):
                    cols = slice(256 * k + 128 * s, 256 * k + 128 * s + 128)
                    w1[512 * r : 512 * r + 512, cols] = w1_ref[r, k, 512 * s : 512 * s + 512, :]
        for c in range(8):
            p0, p1 = w2_ref[0, 2 * c], w2_ref[0, 2 * c + 1]
            cols = slice(128 * c, 128 * c + 128)
            w2[0:256, cols] = jnp.concatenate([p0[:, :64], p1[:, :64]], 1)
            w2[256:512, cols] = jnp.concatenate([p0[:, 64:], p1[:, 64:]], 1)
        pre = jnp.dot(h2[...], w1[...], preferred_element_type=f32) + b1_ref[...]
        act, slope = gelu_parts(pre)
        act = act.astype(bf16)
        dact = lax.dot_general(dm[...], w2[...], NT, preferred_element_type=f32)
        dpre = (dact * slope).astype(bf16)
        dpre_sc[...] = dpre
        gb1_ref[...] = jnp.sum(dpre.astype(f32), axis=0, keepdims=True)
        y = jnp.dot(act, w2[...], preferred_element_type=f32)
        dh = lax.dot_general(dpre, w1[...], NT, preferred_element_type=f32)

        @pl.when(step == 0)
        def _():
            y_acc[...] = y
            dmid_ref[...] = dh

        @pl.when(step > 0)
        def _():
            y_acc[...] += y
            dmid_ref[...] += dh

        g2_sc[...] = lax.dot_general(act, dm[...], TN, preferred_element_type=f32).astype(bf16)

    def grad_1(rows):
        g1 = lax.dot_general(h2[:, rows], dpre_sc[...], TN, preferred_element_type=f32).astype(bf16)
        for ref, swap in ((m1_ref, 0), (t1_ref, 1)):
            for s in range(2):
                ref[0, 0, 512 * s : 512 * s + 512, :] = jnp.where(
                    tab[32] == swap,
                    g1[:, 128 * s : 128 * s + 128],
                    g1[:, 256 + 128 * s : 384 + 128 * s],
                )

    def grad_2(x):
        for z in range(4):
            cols = slice(128 * (2 * z + x), 128 * (2 * z + x) + 128)
            top, low = g2_sc[0:256, cols], g2_sc[256:512, cols]
            even = jnp.concatenate([top[:, :64], low[:, :64]], 1)
            odd = jnp.concatenate([top[:, 64:], low[:, 64:]], 1)
            at = tab[35 + z]
            m2_ref[0, at] = jnp.where(tab[32] == 0, even, odd)
            t2_ref[0, at] = jnp.where(tab[32] == 0, odd, even)

    for i in range(2):

        @pl.when(inner == i)
        def _(i=i):
            grad_1(slice(512 * i, 512 * i + 512))
            grad_2(i)

    @pl.when((step == last) & (inner == 1))
    def _():
        gain2 = vec_ref[1:2, :]
        sums = [jnp.zeros((1, D), f32) for _ in range(4)]
        for rows in pieces:
            out_ref[rows, :] = (mid[rows, :] + (y_acc[rows, :] + vec_ref[3:4, :])).astype(bf16)
            normed, inverse = row_stats(mid[rows, :])
            e = dmid_ref[rows, :]
            scaled = e * gain2
            first = jnp.mean(scaled, axis=-1, keepdims=True)
            second = jnp.mean(scaled * normed, axis=-1, keepdims=True)
            grad = cot_ref[rows, :] + inverse * (scaled - first - normed * second)
            dmid_ref[rows, :] = grad
            branch = grad.astype(bf16)
            h2[rows, :] = branch
            for i, term in enumerate((e * normed, e, branch.astype(f32), dm[rows, :].astype(f32))):
                sums[i] = sums[i] + jnp.sum(term, axis=0, keepdims=True)
        gvec_ref[...] = jnp.concatenate(sums + [jnp.zeros((4, D), f32)], 0)
        datt_ref[...] = lax.dot_general(h2[...], wp[...], NT, preferred_element_type=f32).astype(bf16)
        gp = jnp.dot(o_ref[...], h2[...], preferred_element_type=f32).astype(bf16)
        for r in range(2):
            for c in range(8):
                top = gp[512 * r : 512 * r + 256, 128 * c : 128 * c + 128]
                low = gp[512 * r + 256 : 512 * r + 512, 128 * c : 128 * c + 128]
                gp_ref[r * 16 + 2 * c] = jnp.concatenate([top[:, :64], low[:, :64]], 1)
                gp_ref[r * 16 + 2 * c + 1] = jnp.concatenate([top[:, 64:], low[:, 64:]], 1)


def feed_call(mixed, x_own, cot, table, gathered, bias1, vectors):
    tok = x_own.shape[0]
    by_block = gathered.reshape(2, 16, ROWS_B, 128)
    zero2 = lambda j, i, t: (0, 0)
    zero3 = lambda j, i, t: (0, 0, 0)
    blocks = jax.ShapeDtypeStruct((4, 4, ROWS_FC, 128), bf16)

    def out_1(k):
        return pl.BlockSpec(
            (1, 1, ROWS_FC, 128),
            lambda j, i, t: (t[k * 16 + i * 8 + j] // 4, t[k * 16 + i * 8 + j] % 4, 0, 0),
        )

    def out_2(k):
        return pl.BlockSpec(
            (1, 4, 256, 128), lambda j, i, t: (t[k * 16 + (j // 4) * 8 + i] // 4, 0, j % 4, 0)
        )

    return pl.pallas_call(
        functools.partial(feed_body, tok),
        out_shape=(
            jax.ShapeDtypeStruct((tok, D), bf16),
            jax.ShapeDtypeStruct((tok, D), f32),
            jax.ShapeDtypeStruct((tok, D), bf16),
            jax.ShapeDtypeStruct((32, ROWS_PROJ, 128), bf16),
            blocks,
            blocks,
            blocks,
            blocks,
            jax.ShapeDtypeStruct((1, FF), f32),
            jax.ShapeDtypeStruct((8, D), f32),
        ),
        grid_spec=pltpu.PrefetchScalarGridSpec(
            num_scalar_prefetch=1,
            grid=(8, 2),
            in_specs=[
                once((D, tok), zero2),
                once((tok, D), zero2),
                once((tok, D), zero2),
                once((32, ROWS_PROJ, 128), lambda j, i, t: (0, 8, 0)),
                pl.BlockSpec((2, 2, ROWS_FC, 128), lambda j, i, t: (0, j, 0, 0)),
                pl.BlockSpec((1, 16, 256, 128), lambda j, i, t: (j // 4, 0, 4 + j % 4, 0)),
                pl.BlockSpec((1, 512), lambda j, i, t: (0, j)),
                once((8, D), zero2),
            ],
            out_specs=[
                once((tok, D), zero2),
                once((tok, D), zero2),
                once((tok, D), zero2),
                once((32, ROWS_PROJ, 128), zero3),
                out_1(0),
                out_1(1),
                out_2(0),
                out_2(1),
                pl.BlockSpec((1, 512), lambda j, i, t: (0, j)),
                once((8, D), zero2),
            ],
            scratch_shapes=[
                pltpu.VMEM((tok, D), f32),
                pltpu.VMEM((tok, D), bf16),
                pltpu.VMEM((tok, D), bf16),
                pltpu.VMEM((tok, D), f32),
                pltpu.VMEM((D, 512), bf16),
                pltpu.VMEM((512, D), bf16),
                pltpu.VMEM((D, D), bf16),
                pltpu.VMEM((tok, 512), bf16),
                pltpu.VMEM((512, D), bf16),
            ],
        ),
        compiler_params=params(),
        cost_estimate=cost(2 * tok * D * (6 * FF + 3 * D), 60e6, tok * FF * 2),
        name="feed_forward_both",
    )(table, mixed, x_own, cot, gathered, by_block, by_block, bias1, vectors)


def project_back_body(tok, tab, d0, d1, d2, x_own, x_oth, w00, w01, w10, w11, gain,
                      own_ref, oth_ref, gbias_ref, gvec_ref, w_sc, acc):
    step = pl.program_id(0)
    assemble_qkv(tab[32], ((w00, w01), (w10, w11)), w_sc)
    tile = jnp.concatenate([d0[...], d1[...], d2[...]], 1)
    gbias_ref[...] = jnp.sum(tile.astype(f32), axis=0, keepdims=True)

    @pl.when(step == 0)
    def _():
        acc[0:tok, :] = lax.dot_general(tile[0:tok], w_sc[...], NT, preferred_element_type=f32)
        acc[tok : 2 * tok, :] = jnp.zeros((tok, D), f32)

    @pl.when(step == 1)
    def _():
        acc[0:tok, :] += lax.dot_general(tile[0:tok], w_sc[...], NT, preferred_element_type=f32)

    @pl.when(step >= 2)
    def _():
        acc[...] += lax.dot_general(tile, w_sc[...], NT, preferred_element_type=f32)

    @pl.when(step == pl.num_programs(0) - 1)
    def _():
        first = jnp.zeros((1, D), f32)
        second = jnp.zeros((1, D), f32)
        for half, x_ref in enumerate((x_own, x_oth)):
            for i in range(tok // 112):
                rows = slice(i * 112, (i + 1) * 112)
                e = acc[half * tok + i * 112 : half * tok + (i + 1) * 112, :]
                normed, _ = row_stats(x_ref[rows, :].astype(f32))
                first = first + jnp.sum(e * normed, axis=0, keepdims=True)
                second = second + jnp.sum(e, axis=0, keepdims=True)
                if half == 0:
                    own_ref[rows, :] = e
                else:
                    oth_ref[rows, :] = e.astype(bf16)
        gvec_ref[...] = jnp.concatenate([first, second, jnp.zeros((6, D), f32)], 0)


def project_back_call(dqkv, x_own, x_oth, table, mine, theirs, gain):
    tok = x_own.shape[0]

    def weight(r, k):
        return pl.BlockSpec((1, ROWS_A, 128), lambda j, t: (t[k * 16 + r * 8 + j], 0, 0))

    def piece(i):
        return pl.BlockSpec((None, 2 * tok, 128), lambda j, t: ((3 * j + i) // 8, 0, (3 * j + i) % 8))

    zero2 = lambda j, t: (0, 0)
    return pl.pallas_call(
        functools.partial(project_back_body, tok),
        out_shape=(
            jax.ShapeDtypeStruct((tok, D), f32),
            jax.ShapeDtypeStruct((tok, D), bf16),
            jax.ShapeDtypeStruct((1, 3 * D), f32),
            jax.ShapeDtypeStruct((8, D), f32),
        ),
        grid_spec=pltpu.PrefetchScalarGridSpec(
            num_scalar_prefetch=1,
            grid=(8,),
            in_specs=[
                piece(0),
                piece(1),
                piece(2),
                once((tok, D), zero2),
                once((tok, D), zero2),
                weight(0, 0),
                weight(0, 1),
                weight(1, 0),
                weight(1, 1),
                once((1, D), zero2),
            ],
            out_specs=[
                once((tok, D), zero2),
                once((tok, D), zero2),
                pl.BlockSpec((1, 384), lambda j, t: (0, j)),
                once((8, D), zero2),
            ],
            scratch_shapes=[pltpu.VMEM((D, 384), bf16), pltpu.VMEM((2 * tok, D), f32)],
        ),
        compiler_params=params(),
        cost_estimate=cost(2 * tok * D * D * 5, 24e6),
        name="qkv_backward_tokens",
    )(table, dqkv, dqkv, dqkv, x_own, x_oth, mine, theirs, mine, theirs, gain)


def project_grad_body(tok, tab, h_ref, d0, d1, d2, vec_ref, mine_ref, theirs_ref):
    step = pl.program_id(0)

    def write(rows):
        tile = jnp.concatenate([d0[0:rows], d1[0:rows], d2[0:rows]], 1)
        g = lax.dot_general(h_ref[0:rows, :], tile, TN, preferred_element_type=f32).astype(bf16)
        lo, hi = g[0:256], g[256:512]
        first = (g[:, 0:128], jnp.concatenate([lo[:, 128:192], hi[:, 128:192]], 1))
        second = (g[:, 192:320], jnp.concatenate([lo[:, 320:384], hi[:, 320:384]], 1))
        for ref, swap in ((mine_ref, 0), (theirs_ref, 1)):
            even = tab[32] == swap
            ref[0, 0:512] = jnp.where(even, first[0], second[0])
            ref[0, 512:768] = jnp.where(even, first[1], second[1])
            ref[0, 768:784] = jnp.where(even, vec_ref[0, 0], vec_ref[0, 1])

    @pl.when(step < 2)
    def _():
        write(tok)

    @pl.when(step >= 2)
    def _():
        write(2 * tok)


def project_grad_call(hidden, dqkv, table, packed_vectors):
    both = hidden.shape[0]
    tok = both // 2

    def piece(i):
        return pl.BlockSpec(
            (None, both, 128), lambda j, r, t: ((3 * j + i) // 8, 0, (3 * j + i) % 8)
        )

    def out(k):
        return pl.BlockSpec((1, ROWS_A, 128), lambda j, r, t: (t[k * 16 + r * 8 + j], 0, 0))

    return pl.pallas_call(
        functools.partial(project_grad_body, tok),
        out_shape=(jax.ShapeDtypeStruct((16, ROWS_A, 128), bf16),) * 2,
        grid_spec=pltpu.PrefetchScalarGridSpec(
            num_scalar_prefetch=1,
            grid=(8, 2),
            in_specs=[
                pl.BlockSpec((both, 512), lambda j, r, t: (0, r)),
                piece(0),
                piece(1),
                piece(2),
                pl.BlockSpec((1, 2, 16, 128), lambda j, r, t: (r, j, 0, 0)),
            ],
            out_specs=[out(0), out(1)],
        ),
        compiler_params=params(),
        cost_estimate=cost(2 * tok * D * D * 5, 20e6),
        name="qkv_backward_weights",
    )(table, hidden, dqkv, dqkv, dqkv, packed_vectors)


def finish_body(own_ref, recv_ref, dmid_ref, x_ref, gain, out_ref):
    e = own_ref[...] + recv_ref[...].astype(f32)
    normed, inverse = row_stats(x_ref[...].astype(f32))
    scaled = e * gain[...]
    first = jnp.mean(scaled, axis=-1, keepdims=True)
    second = jnp.mean(scaled * normed, axis=-1, keepdims=True)
    out_ref[...] = dmid_ref[...] + inverse * (scaled - first - normed * second)


def finish_call(own, recv, dmid, x_own, gain):
    tok = own.shape[0]
    block = pl.BlockSpec((112, D), lambda i: (i, 0))
    return pl.pallas_call(
        finish_body,
        out_shape=jax.ShapeDtypeStruct((tok, D), f32),
        grid=(tok // 112,),
        in_specs=[block, block, block, block, pl.BlockSpec((1, D), lambda i: (0, 0))],
        out_specs=block,
        compiler_params=params(),
        cost_estimate=cost(tok * D * 20, 13e6),
        name="first_norm_backward",
    )(own, recv, dmid, x_own, gain)


AXES = ("row", "col")


def spot(y, z, x, core):
    return y * 16 + z * 4 + x * 2 + core


def pairs_of(move):
    return [
        (spot(y, z, x, k), spot(*move(y, z, x, k)))
        for y in range(2)
        for z in range(4)
        for x in range(2)
        for k in range(2)
    ]


def along_z(d):
    return pairs_of(lambda y, z, x, k: (y, z ^ d, x, k))


SECOND = pairs_of(lambda y, z, x, k: (y, z, x ^ 1, k) if k == 0 else (y ^ 1, z, x, k))
THIRD = pairs_of(lambda y, z, x, k: (y ^ 1, z, x, k) if k == 0 else (y, z, x ^ 1, k))
CORE = pairs_of(lambda y, z, x, k: (y, z, x, k ^ 1))


def send(value, pairs):
    return lax.ppermute(value, AXES, pairs)


def place_table():
    y, c = lax.axis_index("row"), lax.axis_index("col")
    z, x, core = c // 4, (c // 2) % 2, c % 2
    index = jnp.arange(16, dtype=jnp.int32)
    dy = (index // 8) ^ y
    dx = (index % 2) ^ x
    dz = ((index % 8) // 2) ^ z
    even = dy * 8 + dx * 4 + dz
    odd = dx * 8 + dy * 4 + dz
    mine = jnp.where(core == 0, even, odd)
    theirs = jnp.where(core == 0, odd, even)
    rest = jnp.stack([core, y, c // 2]).astype(jnp.int32)
    return jnp.concatenate([mine, theirs, rest, jnp.arange(4, dtype=jnp.int32) ^ z]).astype(jnp.int32)


def gather_blocks(rows):
    group = jnp.stack([rows] + [send(rows, along_z(d)) for d in (1, 2, 3)])
    group = jnp.concatenate([group, send(group, SECOND)])
    group = jnp.concatenate([group, send(group, THIRD)])
    return group, send(group, CORE)


def scatter_blocks(mine, theirs):
    flat = (16,) + mine.shape[-2:]
    mine, theirs = mine.reshape(flat), theirs.reshape(flat)

    def part(arrays, where):
        total = arrays[0][where].astype(f32)
        for array in arrays[1:]:
            total = total + array[where].astype(f32)
        return total.astype(bf16)

    arrays = [mine, send(theirs, CORE)]
    arrays.append(send(part(arrays, slice(8, 16)), THIRD))
    arrays.append(send(part(arrays, slice(4, 8)), SECOND))
    return arrays + [send(part(arrays, d), along_z(d)) for d in (1, 2, 3)]


def swap_rows(value):
    return lax.ppermute(value, "row", [(0, 1), (1, 0)])


def fast_device(
    tokens, w_qkv, w_proj, w_fc1, w_fc2, ln1_gain, ln1_bias, q_bias, v_bias,
    proj_bias, ln2_gain, ln2_bias, fc1_bias, fc2_bias, cotangent,
):
    small = (ln1_gain, ln1_bias, q_bias, v_bias, proj_bias, ln2_gain, ln2_bias, fc2_bias)
    vec_rows = jnp.concatenate(small + (fc1_bias,)).reshape(3, 128)
    table = place_table()
    mine_a, theirs_a = gather_blocks(pack_a(w_qkv, jnp.pad(vec_rows, ((0, 13), (0, 0)))))
    x_oth = swap_rows(tokens)
    full_b = lax.all_gather(pack_b(w_fc1, w_fc2, w_proj), AXES, axis=0, tiled=False)
    both = jnp.concatenate([mine_a[:, ROWS_QKV : ROWS_QKV + 3], theirs_a[:, ROWS_QKV : ROWS_QKV + 3]])
    index = jnp.arange(32, dtype=jnp.int32)
    core_of, row_of, chip_of = (index // 2) % 2, index % 2, index // 4
    source = table[row_of * 8 + chip_of + 16 * (core_of != table[32])] + 16 * (core_of != table[32])
    order = (source[:, None] == index[None, :]).astype(bf16)
    vecs = jnp.dot(order, both.reshape(32, 384), preferred_element_type=f32)
    flat = vecs[:, :256].reshape(32, 8, 32).transpose(1, 0, 2).reshape(8, D)
    bias1 = vecs[:, 256:].reshape(1, FF)
    gain1, shift1, bias_q, bias_v = (flat[i : i + 1] for i in range(4))
    qkv_bias = jnp.concatenate([bias_q, jnp.zeros_like(bias_q), bias_v], axis=1)
    second = jnp.concatenate([flat[4:8], jnp.zeros((4, D), f32)], axis=0)

    hidden, qkv = qkv_call(tokens, x_oth, table, mine_a, theirs_a, gain1, shift1, qkv_bias)
    mixed, logsum = attend_call(qkv, tokens.shape[0])
    out, dmid, datt, grad_p, mine_1, theirs_1, mine_2, theirs_2, gb1, gvec2 = feed_call(
        mixed, tokens, cotangent, table, full_b, bias1, second
    )
    terms_2 = scatter_blocks(mine_2, theirs_2)
    terms_1 = scatter_blocks(mine_1, theirs_1)
    rs_p = lax.psum_scatter(grad_p, AXES, scatter_dimension=0, tiled=False)
    dqkv = attend_back_call(qkv, datt, mixed, logsum)
    own, oth, gbias, gvec1 = project_back_call(dqkv, tokens, x_oth, table, mine_a, theirs_a, gain1)
    recv = swap_rows(oth)
    sums = jnp.concatenate(
        [gvec1[0:2], gbias[:, :D], gbias[:, 2 * D :], gvec2[2:3], gvec2[0:2], gvec2[3:4]], axis=0
    )
    lanes = sums.reshape(8, 16, 2, 32).transpose(2, 1, 0, 3).reshape(2, 16, 2, 128)
    ff_lanes = gb1.reshape(16, 2, 1, 128).transpose(1, 0, 2, 3)
    packed = jnp.concatenate([lanes, ff_lanes, jnp.zeros((2, 16, 13, 128), f32)], axis=2).astype(bf16)
    terms_a = scatter_blocks(*project_grad_call(hidden, dqkv, table, packed))
    grad_inputs = finish_call(own, recv, dmid, tokens, gain1)
    (grad_fc1,) = finish_sum(finish_1_body, terms_1, [(512, 256)], "finish_fc1")
    (grad_fc2,) = finish_sum(finish_2_body, terms_2, [(2048, 64)], "finish_fc2")
    grad_proj = pl.pallas_call(
        finish_p_body,
        out_shape=jax.ShapeDtypeStruct((512, 64), f32),
        compiler_params=params(),
        name="finish_proj",
    )(rs_p)
    grad_qkv, *vec = finish_sum(
        finish_a_body, terms_a, [(512, 192)] + [(1, 32)] * 8 + [(1, 128)], "finish_qkv"
    )
    vec = [value.reshape(-1) for value in vec]
    return (
        out, grad_inputs, grad_qkv, grad_proj, grad_fc1, grad_fc2, *vec[:7], vec[8], vec[7],
    )


def solution(mesh):
    fast = dict(mesh.shape) == {"row": 2, "col": 16}
    return jax.shard_map(
        fast_device if fast else per_device,
        mesh=mesh,
        in_specs=(
            P(("col", "row"), None),
            P("row", "col"),
            P("row", "col"),
            P("row", "col"),
            P("row", "col"),
            P(("col", "row")),
            P(("col", "row")),
            P(("col", "row")),
            P(("col", "row")),
            P(("col", "row")),
            P(("col", "row")),
            P(("col", "row")),
            P(("col", "row")),
            P(("col", "row")),
            P(("col", "row"), None),
        ),
        out_specs=(
            P(("col", "row"), None),
            P(("col", "row"), None),
            P("row", "col"),
            P("row", "col"),
            P("row", "col"),
            P("row", "col"),
            P(("col", "row")),
            P(("col", "row")),
            P(("col", "row")),
            P(("col", "row")),
            P(("col", "row")),
            P(("col", "row")),
            P(("col", "row")),
            P(("col", "row")),
            P(("col", "row")),
        ),
        check_vma=False,
    )
```
